512 devices in a mesh: dp: 4 (over x), expert: 128 (over y, z, core).
Axes of the slice: x: 4, y: 8, z: 8, core: 2. Of those that a mesh axis runs over, the one named last changes fastest.
Arguments:
- tokens: bfloat16 [16384, 2048], P('expert', 'dp'), may hold values from -6 to 6
- expert_ids: int32 [16384, 8], P('expert'), may hold values from 0 to 127, all different within a row; in each aligned block of 128 rows (0 to 127, 128 to 255, ...) at most 12 rows name the same one
- chosen_probs: float32 [16384, 8], P('expert'), may hold values from 0.05 to 1
- gate_weight: bfloat16 [128, 1536, 2048], P('expert', 'dp'), may hold values from -0.125 to 0.125
- up_weight: bfloat16 [128, 1536, 2048], P('expert', 'dp'), may hold values from -0.125 to 0.125
- down_weight: bfloat16 [128, 1536, 2048], P('expert', 'dp'), may hold values from -0.15625 to 0.15625
Outputs:
- mixed: bfloat16 [16384, 2048], P('expert', 'dp')
The draws below stay inside these ranges and needn't reach their ends.
Inputs may be any that keep to these rules, and one draw needn't show every extreme that they name: `expert_ids`: each row names 8 different experts; the 128 rows of one device name each expert at most 12 times, a bound that some block reaches.
All inputs are finite; a program needn't handle non-finite values.
Results may differ from the reference program's by a relative error of at most 0.0058.
Values may be sent and summed in bfloat16 or wider, within the bound.
A program may use at most 128 MiB of HBM per device.

```python
import math
import jax
import jax.numpy as jnp
import numpy as np
from jax import lax

D = 2048
FF = 1536
TOP = 8
TOK_DEV = 128
EXPERTS = 128
CAP = 12
TOKENS = 16384
N_DP = 4
N_EXPERT = 128


def steps_of(rng, dims, shards, low, top_value):
    gain = 1.0
    for axis_at, parts in shards:
        heights = jax.random.uniform(jax.random.fold_in(jax.random.fold_in(rng, 6), axis_at), (parts,), jnp.float32, low / len(shards), top_value / len(shards))
        gain = gain * jnp.repeat(jnp.exp(heights), dims[axis_at] // parts).reshape((-1,) + (1,) * (len(dims) - 1 - axis_at))
    return gain


def assign_block(stream_key, own, number, rows, count, top, most, skew):
    order = jax.random.permutation(stream_key, count)
    heavy_load, common = load_shares(count, rows * top, most, skew, True), load_shares(count, rows * top, most, skew, False)
    places = jnp.arange(count)

    def named(lengths, offset_by):
        used = int((lengths > 0).sum())
        fixed = max(1, used // 4)
        moved = fixed + (places - fixed + offset_by * (used - fixed)) % max(1, count - fixed)
        return jnp.zeros((count,), jnp.int32).at[order[jnp.where(places < fixed, places, moved)]].set(jnp.asarray(lengths, jnp.int32))

    lengths = jnp.where(number % 4 == 0, named(heavy_load, number // 4), named(common, number - number // 4 - 1))
    mixed = jax.random.permutation(jax.random.fold_in(own, 3), count)
    giver, receiver = mixed[0:count // 2 * 2:2], mixed[1:count // 2 * 2:2]
    room = jnp.minimum(lengths[giver] - 1, most - lengths[receiver]) // 2
    room = jnp.where((giver == order[0]) | (receiver == order[0]) | (lengths[receiver] == 0), 0, jnp.maximum(room, 0))
    moved = jax.random.randint(jax.random.fold_in(own, 4), (count // 2,), 0, 1 << 20) % (room + 1)
    lengths = lengths.at[giver].add(-moved).at[receiver].add(moved)
    items = jnp.searchsorted(jnp.cumsum(lengths), jnp.arange(rows * top), side="right").astype(jnp.int32)
    listing = items.reshape(top, rows).T
    listing = listing[jax.random.permutation(jax.random.fold_in(own, 1), rows)]
    offset_by = jax.random.randint(jax.random.fold_in(own, 2), (rows, 1), 0, top)
    return jnp.take_along_axis(listing, (jnp.arange(top)[None, :] + offset_by) % top, axis=1)


def load_shares(amount, total, bound, slope, full):
    weights = [(1 << 20) // math.isqrt(standing ** slope) + 1 for standing in range(1, amount + 1)]
    largest = bound if full else min(bound, max(-(-total // amount), total * weights[0] // sum(weights)))
    least = 1 if total - largest >= amount - 1 else 0
    counts, spare = [largest] + [least] * (amount - 1), total - largest - least * (amount - 1)
    while spare > 0:
        free = [i for i in range(1, amount) if counts[i] < largest] or [i for i in range(1, amount) if counts[i] < bound]
        pool, budget = sum([weights[i] for i in free]), spare
        for i in free:
            extra = min(bound - counts[i], max(1, budget * weights[i] // pool), spare)
            counts[i] = counts[i] + extra
            spare = spare - extra
    return np.array(counts)


def normal_values(own_key, shape, scale, reach, shards=(), kind=jnp.bfloat16):
    drawn = jax.random.normal(own_key, shape, jnp.float32) * scale
    if len(shards) > 0:
        drawn = steps_of(own_key, shape, shards, -0.22, 0.18) * drawn
    return jnp.clip(drawn, min=-reach, max=reach).astype(kind)


def setup_inputs(seed: int = 0) -> dict:
    keys = jax.random.split(jax.random.key(seed), 7)
    tokens = normal_values(keys[0], (TOKENS, D), 1.0, 6.0, ((0, 128), (1, 4)))
    expert_ids_keys = jax.random.split(jax.random.fold_in(keys[1], 1), TOKENS // TOK_DEV)
    expert_ids_turns = jax.random.permutation(jax.random.fold_in(keys[1], 3), TOKENS // TOK_DEV)
    expert_ids = jax.vmap(lambda own, number: assign_block(jax.random.fold_in(keys[1], 2), own, number, TOK_DEV, EXPERTS, TOP, CAP, 2))(expert_ids_keys, expert_ids_turns).reshape((TOKENS, TOP))
    chosen_probs = jnp.clip(jnp.exp(math.log(1.0) - 2.9957323 * jax.random.uniform(keys[2], (TOKENS, TOP), jnp.float32) ** steps_of(keys[2], (TOKENS, TOP), ((0, 128),), -0.2, 0.2)), 0.05, 1.0)
    gate_weight = normal_values(keys[3], (EXPERTS, FF, D), D ** -0.5, 0.125, ((0, 128), (1, 4)))
    up_weight = normal_values(keys[4], (EXPERTS, FF, D), D ** -0.5, 0.125, ((0, 128), (1, 4)))
    down_weight = normal_values(keys[5], (EXPERTS, FF, D), FF ** -0.5, 0.15625, ((0, 128), (1, 4)))
    return {"tokens": tokens, "expert_ids": expert_ids, "chosen_probs": chosen_probs, "gate_weight": gate_weight, "up_weight": up_weight, "down_weight": down_weight}


def reference(tokens, expert_ids, chosen_probs, gate_weight, up_weight, down_weight):
    route = chosen_probs / jnp.sum(chosen_probs, axis=1, keepdims=True)
    ntok = tokens.shape[0]
    width = tokens.shape[1]
    flat = expert_ids.reshape(-1).astype(jnp.int32)
    count = ntok * TOP
    onehot = (flat[:, None] == jnp.arange(EXPERTS, dtype=jnp.int32)[None, :]).astype(jnp.int32)
    blocked = onehot.reshape(N_EXPERT, TOK_DEV * TOP, EXPERTS)
    ranks = (jnp.cumsum(blocked, axis=1) - 1).reshape(count, EXPERTS)
    slot = jnp.sum(onehot * ranks, axis=1).astype(jnp.int32)
    owner = (jnp.arange(count, dtype=jnp.int32) // (TOK_DEV * TOP)).astype(jnp.int32)
    place = ((flat * N_EXPERT + owner) * CAP + slot).astype(jnp.int32)
    table = jnp.zeros((EXPERTS * N_EXPERT * CAP,), jnp.int32).at[place].set(jnp.arange(count, dtype=jnp.int32) + 1)
    table = table.reshape(EXPERTS, N_EXPERT * CAP)
    tok_of = jnp.concatenate([jnp.zeros((1,), jnp.int32), (jnp.arange(count, dtype=jnp.int32) // TOP + 1).astype(jnp.int32)])
    weight_of = jnp.concatenate([jnp.zeros((1,), jnp.float32), route.reshape(-1).astype(jnp.float32)])
    padded = jnp.concatenate([jnp.zeros((1, width), tokens.dtype), tokens], axis=0)
    block = FF // N_DP

    def one_expert(total, items):
        gate_w, up_w, down_w, entries = items
        tok_index = tok_of[entries]
        weights = weight_of[entries]
        rows = padded[tok_index]
        gate = jnp.dot(rows, gate_w.T, preferred_element_type=jnp.float32)
        up = jnp.dot(rows, up_w.T, preferred_element_type=jnp.float32)
        hidden = (jax.nn.silu(gate) * up).astype(jnp.bfloat16)
        for piece in range(N_DP):
            part = jnp.dot(hidden[:, piece * block:(piece + 1) * block], down_w[piece * block:(piece + 1) * block], preferred_element_type=jnp.float32).astype(jnp.bfloat16)
            total = total.at[tok_index].add(part.astype(jnp.float32) * weights[:, None])
        return total, None

    start = jnp.zeros((ntok + 1, width), jnp.float32)
    total, _ = lax.scan(one_expert, start, (gate_weight, up_weight, down_weight, table))
    return total[1:].astype(jnp.bfloat16)
```

```python
import functools

import jax
import jax.numpy as jnp
from jax import lax
from jax.experimental import pallas as pl
from jax.experimental.pallas import tpu as pltpu
from jax.sharding import PartitionSpec as P

LANES = 128
CAP = 12
TILE = 16
TILES = 3
ROWS = TILE * TILES
F32 = jnp.float32
BF16 = jnp.bfloat16


def wanted_slot(tile, row):
    return jnp.where(row < CAP, row, row - CAP + 4 * tile)


def pack_kernel(ids_ref, tok_ref, out_ref):
    tokens = tok_ref.shape[0]
    experts = out_ref.shape[0]
    which = lax.broadcasted_iota(jnp.int32, (experts, tokens), 0)
    chosen = jnp.zeros((experts, tokens), F32)
    for k in range(ids_ref.shape[0]):
        chosen = chosen + (which == ids_ref[k : k + 1, :]).astype(F32)
    before = lax.broadcasted_iota(jnp.int32, (tokens, tokens), 0)
    after = lax.broadcasted_iota(jnp.int32, (tokens, tokens), 1)
    upper = (before < after).astype(F32).astype(BF16)
    rank = jnp.dot(chosen.astype(BF16), upper, preferred_element_type=F32)
    slot = jnp.where(chosen > 0.0, rank, -1.0).astype(jnp.int32)
    block = min(16, experts)
    row = lax.broadcasted_iota(jnp.int32, (block, TILE, tokens), 1)
    rows2 = lax.broadcasted_iota(jnp.int32, (block, TILE, LANES), 1)
    for start in range(0, experts, block):
        mine = jnp.broadcast_to(slot[start : start + block][:, None, :], (block, TILE, tokens))
        for tile in range(TILES):
            pick = (mine == wanted_slot(tile, row)).astype(F32).astype(BF16)
            pick = pick.reshape(block * TILE, tokens)
            source = jnp.concatenate(
                [tok_ref[:, tile * LANES : (tile + 1) * LANES], tok_ref[:, TILES * LANES :]], axis=1
            )
            got = jnp.dot(pick, source, preferred_element_type=F32)
            main = got[:, :LANES].reshape(block, TILE, LANES)
            rest = got[:, LANES:].reshape(block, TILE, LANES)
            out_ref[start : start + block, tile * TILE : (tile + 1) * TILE, :] = jnp.where(
                rows2 < CAP, main, rest
            ).astype(BF16)


def grid_place(nz):
    e = lax.axis_index("expert")
    core = lax.rem(e, 2)
    z = lax.rem(lax.div(e, 2), nz)
    y = lax.div(e, 2 * nz)
    return e, y, z, core


def peer_of(k, sign, place, ny, nz):
    _, y, z, core = place
    group = lax.div(k, 2 * nz)
    item = lax.rem(k, 2 * nz)
    dz = lax.div(item, 2)
    dc = lax.rem(item, 2)
    dy = lax.rem(dz + group, ny)
    if sign > 0:
        y2, z2 = lax.rem(y + dy, ny), lax.rem(z + dz, nz)
    else:
        y2, z2 = lax.rem(y + ny - dy, ny), lax.rem(z + nz - dz, nz)
    return (y2 * nz + z2) * 2 + lax.rem(core + dc, 2)


def remote(src, dst, send, recv, device):
    return pltpu.make_async_remote_copy(
        src_ref=src,
        dst_ref=dst,
        send_sem=send,
        recv_sem=recv,
        device_id=device,
        device_id_type=pl.DeviceIdType.MESH,
    )


def enter(place, n, ny, nz, right, left):
    barrier = pltpu.get_barrier_semaphore()

    def greet(k, carry):
        pl.semaphore_signal(
            barrier,
            inc=1,
            device_id={"expert": peer_of(k, 1, place, ny, nz)},
            device_id_type=pl.DeviceIdType.MESH,
        )
        return carry

    lax.fori_loop(1, n, greet, 0)
    for side in (right, left):
        pl.semaphore_signal(
            barrier, inc=1, device_id={"dp": side}, device_id_type=pl.DeviceIdType.MESH
        )
    pl.semaphore_wait(barrier, n + 1)


def dispatch_kernel(ny, nz, packed, out, own_sem, send_sem, recv_sem, xsend, lsem, rsem, fsem):
    n = 2 * ny * nz
    per = 2 * nz
    x = lax.axis_index("dp")
    place = grid_place(nz)
    e = place[0]
    right, left = lax.rem(x + 1, 4), lax.rem(x + 3, 4)
    enter(place, n, ny, nz, right, left)

    own = pltpu.make_async_copy(packed.at[e], out.at[x, 0], own_sem)
    own.start()
    for g in range(ny):

        def send(k, carry, g=g):
            dest = peer_of(k, 1, place, ny, nz)
            remote(
                packed.at[dest], out.at[x, k], send_sem, recv_sem.at[g], {"expert": dest}
            ).start()
            return carry

        lax.fori_loop(max(1, g * per), (g + 1) * per, send, 0)
    own.wait()

    def part(q, g):
        return out.at[q, pl.ds(g * per, per)]

    def forward(g):
        if g % 2 == 0:
            remote(part(left, g), part(left, g), xsend, lsem.at[g], {"dp": right}).wait_recv()
            remote(part(left, g), part(left, g), xsend, fsem.at[g], {"dp": right}).start()
        else:
            remote(part(right, g), part(right, g), xsend, rsem.at[g], {"dp": left}).wait_recv()
            remote(part(right, g), part(right, g), xsend, fsem.at[g], {"dp": left}).start()

    for g in range(ny):
        first = 1 if g == 0 else 0
        whole = out.at[x, pl.ds(g * per + first, per - first)]
        remote(whole, whole, send_sem, recv_sem.at[g], {"dp": right}).wait_recv()
        remote(part(x, g), part(x, g), xsend, lsem.at[g], {"dp": right}).start()
        remote(part(x, g), part(x, g), xsend, rsem.at[g], {"dp": left}).start()
        if g >= 1:
            forward(g - 1)
    forward(ny - 1)
    far = lax.rem(x + 2, 4)
    for g in range(ny):
        if g % 2 == 0:
            remote(part(right, g), part(right, g), xsend, rsem.at[g], {"dp": left}).wait_recv()
        else:
            remote(part(left, g), part(left, g), xsend, lsem.at[g], {"dp": right}).wait_recv()
        remote(part(far, g), part(far, g), xsend, fsem.at[g], {"dp": right}).wait_recv()
    sent = packed.at[pl.ds(0, n - 1)]
    remote(sent, sent, send_sem, recv_sem.at[0], {"dp": right}).wait_send()
    three = out.at[pl.ds(0, 3)]
    remote(three, three, xsend, recv_sem.at[0], {"dp": right}).wait_send()


def expert_kernel(in_ref, gate_ref, up_ref, down_ref, out_ref, rows_ref):
    parts, batch = in_ref.shape[0], in_ref.shape[1]
    rows = batch * TILE
    half = TILE // 2
    low = lax.broadcasted_iota(jnp.int32, (batch, half, LANES), 1) < half // 2
    for q in range(parts):
        uppers = []
        base = q * (TILES + 1) * LANES
        for tile in range(TILES):
            value = in_ref[q, :, tile * TILE : (tile + 1) * TILE, :]
            rows_ref[:, base + tile * LANES : base + (tile + 1) * LANES] = value.reshape(rows, LANES)
            uppers.append(value.astype(F32)[:, half:, :])
        first = jnp.where(low, pltpu.roll(uppers[0], half // 2, 1), uppers[1])
        second = pltpu.roll(uppers[2], half // 2, 1)
        last = jnp.concatenate([first, second], axis=1).reshape(rows, LANES).astype(BF16)
        rows_ref[:, base + TILES * LANES : base + (TILES + 1) * LANES] = last
    dims = (((1,), (1,)), ((), ()))
    gate = lax.dot_general(rows_ref[...], gate_ref[0], dims, preferred_element_type=F32)
    up = lax.dot_general(rows_ref[...], up_ref[0], dims, preferred_element_type=F32)
    hidden = (gate / (1.0 + jnp.exp(-gate)) * up).astype(BF16)
    for q in range(parts):
        base = q * (TILES + 1) * LANES
        made = jnp.dot(
            hidden, down_ref[0, :, base : base + (TILES + 1) * LANES], preferred_element_type=F32
        )
        last = made[:, TILES * LANES :].reshape(batch, TILE, LANES)
        fill = (
            pltpu.roll(last[:, :half], half // 2, 1),
            last[:, :half],
            pltpu.roll(last[:, half:], half // 2, 1),
        )
        for tile in range(TILES):
            main = made[:, tile * LANES : (tile + 1) * LANES].reshape(batch, TILE, LANES)
            upper = jnp.where(low, main[:, half:], fill[tile])
            out_ref[q, :, tile * TILE : (tile + 1) * TILE, :] = jnp.concatenate(
                [main[:, :half], upper], axis=1
            ).astype(BF16)


def return_kernel(
    ny, nz, made, ret,
    own, near, diag, from_left, from_right, passed, total,
    own_sem, near_sem, dsem, lsem, rsem, xsend, send_sem, ret_sem, last_sem,
):
    n = 2 * ny * nz
    per = 2 * nz
    x = lax.axis_index("dp")
    place = grid_place(nz)
    e = place[0]
    right, left, far = lax.rem(x + 1, 4), lax.rem(x + 3, 4), lax.rem(x + 2, 4)

    def part(q, g):
        return made.at[q, pl.ds(g * per, per)]

    def stage_own(g):
        return pltpu.make_async_copy(part(x, g), own.at[g], own_sem.at[g])

    def stage_near(g):
        side = right if g % 2 == 0 else left
        return pltpu.make_async_copy(part(side, g), near.at[g], near_sem.at[g])

    for g in range(ny):
        stage_near(g).start()
        stage_own(g).start()
    enter(place, n, ny, nz, right, left)

    def issue(g):
        if g % 2 == 0:
            remote(part(far, g), diag.at[g], xsend, dsem.at[g], {"dp": right}).start()
            remote(part(left, g), from_right.at[g], xsend, rsem.at[g], {"dp": left}).start()
        else:
            remote(part(far, g), diag.at[g], xsend, dsem.at[g], {"dp": left}).start()
            remote(part(right, g), from_left.at[g], xsend, lsem.at[g], {"dp": right}).start()

    def forward(g):
        stage_near(g).wait()
        remote(diag.at[g], diag.at[g], xsend, dsem.at[g], {"dp": right}).wait_recv()
        passed[g] = (diag[g].astype(F32) + near[g].astype(F32)).astype(BF16)
        if g % 2 == 0:
            remote(passed.at[g], from_left.at[g], xsend, lsem.at[g], {"dp": right}).start()
        else:
            remote(passed.at[g], from_right.at[g], xsend, rsem.at[g], {"dp": left}).start()

    def finish(g):
        stage_own(g).wait()
        remote(from_left.at[g], from_left.at[g], xsend, lsem.at[g], {"dp": right}).wait_recv()
        remote(from_right.at[g], from_right.at[g], xsend, rsem.at[g], {"dp": right}).wait_recv()
        total[g] = (
            own[g].astype(F32) + from_left[g].astype(F32) + from_right[g].astype(F32)
        ).astype(BF16)

        def send(i, carry):
            dest = peer_of(g * per + i, -1, place, ny, nz)
            remote(total.at[g, i], ret.at[e], send_sem, ret_sem, {"expert": dest}).start()
            return carry

        lax.fori_loop(1 if g == 0 else 0, per, send, 0)
        if g == 0:
            pltpu.make_async_copy(total.at[0, 0], ret.at[e], last_sem).start()

    ahead = min(ny, 4)
    for g in range(ahead):
        issue(g)
    for g in range(0, ny, 2):
        forward(g)
        forward(g + 1)
        for h in (g + ahead, g + ahead + 1):
            if h < ny:
                issue(h)
        if g >= 2:
            finish(g - 2)
            finish(g - 1)
    finish(ny - 2)
    finish(ny - 1)
    pltpu.make_async_copy(total.at[0, 0], ret.at[e], last_sem).wait()
    most = ret.at[pl.ds(0, n - 1)]
    remote(most, most, send_sem, ret_sem, {"dp": right}).wait()
    three = made.at[pl.ds(0, 3)]
    remote(three, three, xsend, ret_sem, {"dp": right}).wait_send()


def combine_kernel(ids_ref, probs_ref, ret_ref, out_ref):
    tokens, top = ids_ref.shape
    experts = ret_ref.shape[0]
    probs = probs_ref[...]
    route = probs / jnp.sum(probs, axis=1, keepdims=True)
    ids = ids_ref[...]
    which = lax.broadcasted_iota(jnp.int32, (tokens, experts), 1)
    chosen = jnp.zeros((tokens, experts), F32)
    weight = jnp.zeros((tokens, experts), F32)
    for k in range(top):
        hit = which == ids[:, k : k + 1]
        chosen = chosen + hit.astype(F32)
        weight = weight + jnp.where(hit, route[:, k : k + 1], 0.0)
    here = lax.broadcasted_iota(jnp.int32, (tokens, tokens), 0)
    other = lax.broadcasted_iota(jnp.int32, (tokens, tokens), 1)
    lower = (other < here).astype(F32).astype(BF16)
    rank = jnp.dot(lower, chosen.astype(BF16), preferred_element_type=F32)
    slot = jnp.where(chosen > 0.0, rank, -1.0).astype(BF16)
    high = weight.astype(BF16)
    rest = (weight - high.astype(F32)).astype(BF16)
    wide = experts * TILE
    column = lax.broadcasted_iota(jnp.int32, (experts, wide), 1)
    line = lax.broadcasted_iota(jnp.int32, (experts, wide), 0)
    spread = ((column >= line * TILE) & (column < line * TILE + TILE)).astype(F32).astype(BF16)
    slots = jnp.dot(slot, spread, preferred_element_type=F32).astype(jnp.int32)
    highs = jnp.dot(high, spread, preferred_element_type=F32)
    rests = jnp.dot(rest, spread, preferred_element_type=F32)
    row = lax.broadcasted_iota(jnp.int32, (tokens, wide), 1) & (TILE - 1)
    last = jnp.zeros((tokens, LANES), F32)
    for tile in range(TILES):
        hit = slots == wanted_slot(tile, row)
        masks = (hit & (row < CAP), hit & (row >= CAP))
        left = jnp.concatenate(
            [jnp.where(m, w, 0.0).astype(BF16) for m in masks for w in (highs, rests)], axis=0
        )
        right = ret_ref[:, tile * TILE : (tile + 1) * TILE, :].reshape(wide, LANES)
        got = jnp.dot(left, right, preferred_element_type=F32)
        out_ref[:, tile * LANES : (tile + 1) * LANES] = (
            got[:tokens] + got[tokens : 2 * tokens]
        ).astype(BF16)
        last = last + got[2 * tokens : 3 * tokens] + got[3 * tokens :]
    out_ref[:, TILES * LANES :] = last.astype(BF16)


def vmem(count):
    return [pl.BlockSpec(memory_space=pltpu.VMEM)] * count


ANYWHERE = pl.BlockSpec(memory_space=pl.ANY)


def local(ny, nz, tokens, expert_ids, chosen_probs, gate_weight, up_weight, down_weight):
    n = 2 * ny * nz
    per = 2 * nz
    dma = pltpu.SemaphoreType.DMA
    packed = pl.pallas_call(
        pack_kernel,
        out_shape=jax.ShapeDtypeStruct((n, ROWS, LANES), BF16),
        in_specs=vmem(2),
        out_specs=vmem(1)[0],
        name="pack",
    )(expert_ids.T, tokens)
    arrived = pl.pallas_call(
        functools.partial(dispatch_kernel, ny, nz),
        out_shape=jax.ShapeDtypeStruct((4, n, ROWS, LANES), BF16),
        in_specs=[ANYWHERE],
        out_specs=ANYWHERE,
        scratch_shapes=[
            dma(()), dma(()), dma((ny,)), dma(()), dma((ny,)), dma((ny,)), dma((ny,)),
        ],
        compiler_params=pltpu.CompilerParams(collective_id=0, has_side_effects=True),
        name="dispatch",
    )(packed)
    ff, width = gate_weight.shape[1], gate_weight.shape[2]
    batch = min(32, n)
    block = pl.BlockSpec((4, batch, ROWS, LANES), lambda i: (0, i, 0, 0))
    whole = pl.BlockSpec((1, ff, width), lambda i: (0, 0, 0), pipeline_mode=pl.Buffered(1))
    made = pl.pallas_call(
        expert_kernel,
        grid=(n // batch,),
        out_shape=jax.ShapeDtypeStruct((4, n, ROWS, LANES), BF16),
        in_specs=[block, whole, whole, whole],
        out_specs=block,
        scratch_shapes=[pltpu.VMEM((batch * TILE, width), BF16)],
        name="expert",
    )(arrived, gate_weight, up_weight, down_weight)
    held = pltpu.VMEM((ny, per, ROWS, LANES), BF16)
    back = pl.pallas_call(
        functools.partial(return_kernel, ny, nz),
        out_shape=jax.ShapeDtypeStruct((n, ROWS, LANES), BF16),
        in_specs=[ANYWHERE],
        out_specs=ANYWHERE,
        scratch_shapes=[held] * 7
        + [dma((ny,))] * 5
        + [dma(()), dma(()), dma(()), dma(())],
        compiler_params=pltpu.CompilerParams(collective_id=1, has_side_effects=True),
        name="giveback",
    )(made)
    return pl.pallas_call(
        combine_kernel,
        out_shape=jax.ShapeDtypeStruct(tokens.shape, BF16),
        in_specs=vmem(3),
        out_specs=vmem(1)[0],
        name="combine",
    )(expert_ids, chosen_probs, back)


def build(mesh, ny, nz):
    in_specs = (
        P("expert", "dp"),
        P("expert", None),
        P("expert", None),
        P("expert", "dp", None),
        P("expert", "dp", None),
        P("expert", "dp", None),
    )
    return jax.shard_map(
        functools.partial(local, ny, nz),
        mesh=mesh,
        in_specs=in_specs,
        out_specs=P("expert", "dp"),
        check_vma=False,
    )


def solution(mesh):
    return build(mesh, 8, 8)
```

```python
import functools

import jax
import jax.numpy as jnp
from jax import lax
from jax.experimental import pallas as pl
from jax.experimental.pallas import tpu as pltpu
from jax.sharding import PartitionSpec as P

LANES = 128
CAP = 12
TILE = 16
TILES = 3
ROWS = TILE * TILES
F32 = jnp.float32
BF16 = jnp.bfloat16


def wanted_slot(tile, row):
    return jnp.where(row < CAP, row, row - CAP + 4 * tile)


def grid_place(nz):
    e = lax.axis_index("expert")
    core = lax.rem(e, 2)
    z = lax.rem(lax.div(e, 2), nz)
    y = lax.div(e, 2 * nz)
    return e, y, z, core


def peer_of(k, sign, place, ny, nz):
    _, y, z, core = place
    group = lax.div(k, 2 * nz)
    item = lax.rem(k, 2 * nz)
    dz = lax.div(item, 2)
    dc = lax.rem(item, 2)
    dy = lax.rem(dz + group, ny)
    if sign > 0:
        y2, z2 = lax.rem(y + dy, ny), lax.rem(z + dz, nz)
    else:
        y2, z2 = lax.rem(y + ny - dy, ny), lax.rem(z + nz - dz, nz)
    return (y2 * nz + z2) * 2 + lax.rem(core + dc, 2)


def remote(src, dst, send, recv, device):
    return pltpu.make_async_remote_copy(
        src_ref=src,
        dst_ref=dst,
        send_sem=send,
        recv_sem=recv,
        device_id=device,
        device_id_type=pl.DeviceIdType.MESH,
    )


def side_of(x, way):
    return lax.rem(x + 1 + 2 * way, 4)


def route_tables(ids_ref, probs_ref, experts):
    top, tokens = ids_ref.shape
    probs = probs_ref[...]
    route = probs / jnp.sum(probs, axis=0, keepdims=True)
    which = lax.broadcasted_iota(jnp.int32, (experts, tokens), 0)
    chosen = jnp.zeros((experts, tokens), F32)
    weight = jnp.zeros((experts, tokens), F32)
    for k in range(top):
        hit = which == ids_ref[k : k + 1, :]
        chosen = chosen + hit.astype(F32)
        weight = weight + jnp.where(hit, route[k : k + 1, :], 0.0)
    before = lax.broadcasted_iota(jnp.int32, (tokens, tokens), 0)
    after = lax.broadcasted_iota(jnp.int32, (tokens, tokens), 1)
    upper = (before < after).astype(F32).astype(BF16)
    rank = jnp.dot(chosen.astype(BF16), upper, preferred_element_type=F32)
    return jnp.where(chosen > 0.0, rank, -1.0), weight


def pack(slot_ref, tok_ref, packed):
    experts, tokens = slot_ref.shape
    block = min(16, experts)
    row = lax.broadcasted_iota(jnp.int32, (block, TILE, tokens), 1)
    rows2 = lax.broadcasted_iota(jnp.int32, (block, TILE, LANES), 1)

    def step(i, carry):
        start = pl.multiple_of(i * block, block)
        mine = jnp.broadcast_to(slot_ref[pl.ds(start, block), :][:, None, :], (block, TILE, tokens))
        for tile in range(TILES):
            pick = (mine == wanted_slot(tile, row)).astype(F32).astype(BF16)
            pick = pick.reshape(block * TILE, tokens)
            source = jnp.concatenate(
                [tok_ref[:, tile * LANES : (tile + 1) * LANES], tok_ref[:, TILES * LANES :]], axis=1
            )
            got = jnp.dot(pick, source, preferred_element_type=F32)
            main = got[:, :LANES].reshape(block, TILE, LANES)
            rest = got[:, LANES:].reshape(block, TILE, LANES)
            packed[pl.ds(start, block), tile * TILE : (tile + 1) * TILE, :] = jnp.where(
                rows2 < CAP, main, rest
            ).astype(BF16)
        return carry

    lax.fori_loop(0, experts // block, step, 0)


def mixing(slot, weight, mix):
    tokens, experts = slot.shape
    high = weight.astype(BF16)
    rest = (weight - high.astype(F32)).astype(BF16)
    wide = experts * TILE
    column = lax.broadcasted_iota(jnp.int32, (experts, wide), 1)
    line = lax.broadcasted_iota(jnp.int32, (experts, wide), 0)
    spread = ((column >= line * TILE) & (column < line * TILE + TILE)).astype(F32).astype(BF16)
    slots = jnp.dot(slot.astype(BF16), spread, preferred_element_type=F32).astype(jnp.int32)
    highs = jnp.dot(high, spread, preferred_element_type=F32)
    rests = jnp.dot(rest, spread, preferred_element_type=F32)
    row = lax.broadcasted_iota(jnp.int32, (tokens, wide), 1) & (TILE - 1)
    for tile in range(TILES):
        hit = slots == wanted_slot(tile, row)
        masks = (hit & (row < CAP), hit & (row >= CAP))
        for i, (m, w) in enumerate((m, w) for m in masks for w in (highs, rests)):
            mix[tile, i * tokens : (i + 1) * tokens, :] = jnp.where(m, w, 0.0).astype(BF16)


def combine(mix, ret, out_ref):
    tokens = out_ref.shape[0]
    experts = ret.shape[0]
    last = jnp.zeros((tokens, LANES), F32)
    for tile in range(TILES):
        right = ret[:, tile * TILE : (tile + 1) * TILE, :].reshape(experts * TILE, LANES)
        got = jnp.dot(mix[tile], right, preferred_element_type=F32)
        out_ref[:, tile * LANES : (tile + 1) * LANES] = (
            got[:tokens] + got[tokens : 2 * tokens]
        ).astype(BF16)
        last = last + got[2 * tokens : 3 * tokens] + got[3 * tokens :]
    out_ref[:, TILES * LANES :] = last.astype(BF16)


def apply_expert(arrived, made, start, batch, rows_ref, gate_up, down):
    parts = arrived.shape[0]
    ff = down.shape[0]
    rows = batch * TILE
    half = TILE // 2
    low = lax.broadcasted_iota(jnp.int32, (batch, half, LANES), 1) < half // 2
    for q in range(parts):
        uppers = []
        base = q * (TILES + 1) * LANES
        for tile in range(TILES):
            value = arrived[q, pl.ds(start, batch), tile * TILE : (tile + 1) * TILE, :]
            rows_ref[:, base + tile * LANES : base + (tile + 1) * LANES] = value.reshape(rows, LANES)
            uppers.append(value.astype(F32)[:, half:, :])
        first = jnp.where(low, pltpu.roll(uppers[0], half // 2, 1), uppers[1])
        second = pltpu.roll(uppers[2], half // 2, 1)
        last = jnp.concatenate([first, second], axis=1).reshape(rows, LANES).astype(BF16)
        rows_ref[:, base + TILES * LANES : base + (TILES + 1) * LANES] = last
    dims = (((1,), (1,)), ((), ()))
    both = lax.dot_general(rows_ref[...], gate_up[...], dims, preferred_element_type=F32)
    gate, up = both[:, :ff], both[:, ff:]
    hidden = (gate / (1.0 + jnp.exp(-gate)) * up).astype(BF16)
    for q in range(parts):
        base = q * (TILES + 1) * LANES
        result = jnp.dot(
            hidden, down[:, base : base + (TILES + 1) * LANES], preferred_element_type=F32
        )
        last = result[:, TILES * LANES :].reshape(batch, TILE, LANES)
        fill = (
            pltpu.roll(last[:, :half], half // 2, 1),
            last[:, :half],
            pltpu.roll(last[:, half:], half // 2, 1),
        )
        for tile in range(TILES):
            main = result[:, tile * LANES : (tile + 1) * LANES].reshape(batch, TILE, LANES)
            upper = jnp.where(low, main[:, half:], fill[tile])
            made[q, pl.ds(start, batch), tile * TILE : (tile + 1) * TILE, :] = jnp.concatenate(
                [main[:, :half], upper], axis=1
            ).astype(BF16)


def moe_kernel(
    ny, nz, ids_ref, probs_ref, tok_ref, gate_hbm, up_hbm, down_hbm, out_ref,
    gate_up, down, slot_ref, packed, arrived, rows_ref, made, diag, near, passed, total, ret, mix,
    weight_sem, go_send, go_recv, gather_send, side_recv, far_recv,
    sum_send, diag_recv, near_recv, back_send, back_recv, self_sem,
):
    n = 2 * ny * nz
    per = 2 * nz
    ff = down.shape[0]
    x = lax.axis_index("dp")
    place = grid_place(nz)
    e = place[0]
    right, left, far = side_of(x, 0), side_of(x, 1), lax.rem(x + 2, 4)

    weights = (
        pltpu.make_async_copy(gate_hbm.at[0], gate_up.at[pl.ds(0, ff)], weight_sem.at[0]),
        pltpu.make_async_copy(up_hbm.at[0], gate_up.at[pl.ds(ff, ff)], weight_sem.at[1]),
        pltpu.make_async_copy(down_hbm.at[0], down, weight_sem.at[2]),
    )
    for copy in weights:
        copy.start()

    barrier = pltpu.get_barrier_semaphore()

    def greet(k, carry):
        pl.semaphore_signal(
            barrier,
            inc=1,
            device_id={"expert": peer_of(k, 1, place, ny, nz)},
            device_id_type=pl.DeviceIdType.MESH,
        )
        return carry

    for side in (right, left):
        pl.semaphore_signal(
            barrier, inc=1, device_id={"dp": side}, device_id_type=pl.DeviceIdType.MESH
        )
    lax.fori_loop(1, n, greet, 0)

    slot, weight = route_tables(ids_ref, probs_ref, n)
    slot_ref[...] = slot.astype(jnp.int32)
    pack(slot_ref, tok_ref, packed)
    pl.semaphore_wait(barrier, n + 1)

    def send_out(k, carry):
        dest = peer_of(k, 1, place, ny, nz)
        remote(
            packed.at[dest], arrived.at[x, k], go_send, go_recv.at[lax.div(k, per)], {"expert": dest}
        ).start()
        return carry

    own = pltpu.make_async_copy(packed.at[e], arrived.at[x, 0], self_sem.at[0])
    own.start()
    lax.fori_loop(1, n, send_out, 0)
    mixing(slot.T, weight.T, mix)
    for copy in weights:
        copy.wait()
    own.wait()

    def got(q, g):
        return arrived.at[q, pl.ds(g * per, per)]

    def part(q, g):
        return made.at[q, pl.ds(g * per, per)]

    def share(g):
        @pl.when(g == 0)
        def _():
            some = arrived.at[x, pl.ds(1, per - 1)]
            remote(some, some, go_send, go_recv.at[0], {"dp": right}).wait_recv()

        @pl.when(g > 0)
        def _():
            remote(got(x, g), got(x, g), go_send, go_recv.at[g], {"dp": right}).wait_recv()

        for way in (0, 1):
            remote(
                got(x, g), got(x, g), gather_send, side_recv.at[way, g], {"dp": side_of(x, way)}
            ).start()

    def share_on(g):
        way = lax.rem(g, 2)
        block = got(side_of(x, 1 - way), g)
        remote(block, block, gather_send, side_recv.at[way, g], {"dp": right}).wait_recv()
        remote(block, block, gather_send, far_recv.at[g], {"dp": side_of(x, way)}).start()

    def work(g):
        way = lax.rem(g, 2)
        block = got(side_of(x, way), g)
        remote(block, block, gather_send, side_recv.at[1 - way, g], {"dp": right}).wait_recv()
        remote(got(far, g), got(far, g), gather_send, far_recv.at[g], {"dp": right}).wait_recv()
        apply_expert(arrived, made, g * per, per, rows_ref, gate_up, down)
        remote(
            part(far, g), diag.at[g], sum_send, diag_recv.at[g], {"dp": side_of(x, way)}
        ).start()
        other = side_of(x, 1 - way)
        remote(
            part(other, g), near.at[1 - way, g], sum_send, near_recv.at[1 - way, g], {"dp": other}
        ).start()

    def sum_on(g):
        way = lax.rem(g, 2)
        dest = side_of(x, way)
        remote(diag.at[g], diag.at[g], sum_send, diag_recv.at[g], {"dp": right}).wait_recv()
        passed[g] = (
            diag[g].astype(F32) + made[dest, pl.ds(g * per, per)].astype(F32)
        ).astype(BF16)
        remote(
            passed.at[g], near.at[way, g], sum_send, near_recv.at[way, g], {"dp": dest}
        ).start()

    def give_back(g):
        for way in (0, 1):
            block = near.at[way, g]
            remote(block, block, sum_send, near_recv.at[way, g], {"dp": right}).wait_recv()
        total[g] = (
            made[x, pl.ds(g * per, per)].astype(F32)
            + near[0, g].astype(F32)
            + near[1, g].astype(F32)
        ).astype(BF16)

        def send(i, carry):
            dest = peer_of(g * per + i, -1, place, ny, nz)
            remote(total.at[g, i], ret.at[e], back_send, back_recv, {"expert": dest}).start()
            return carry

        @pl.when(g == 0)
        def _():
            pltpu.make_async_copy(total.at[0, 0], ret.at[e], self_sem.at[1]).start()
            lax.fori_loop(1, per, send, 0)

        @pl.when(g > 0)
        def _():
            lax.fori_loop(0, per, send, 0)

    def step(i, carry):
        for stage, late in ((share, 0), (share_on, 1), (sum_on, 3), (work, 2), (give_back, 4)):

            @pl.when((i >= late) & (i < ny + late))
            def _(stage=stage, late=late):
                stage(i - late)

        return carry

    lax.fori_loop(0, ny + 4, step, 0)
    pltpu.make_async_copy(total.at[0, 0], ret.at[e], self_sem.at[1]).wait()
    most = ret.at[pl.ds(0, n - 1)]
    remote(most, most, back_send, back_recv, {"dp": right}).wait_recv()
    combine(mix, ret, out_ref)
    remote(most, most, back_send, back_recv, {"dp": right}).wait_send()
    remote(most, most, go_send, back_recv, {"dp": right}).wait_send()
    three = made.at[pl.ds(0, 3)]
    remote(three, three, gather_send, back_recv, {"dp": right}).wait_send()
    remote(three, three, sum_send, back_recv, {"dp": right}).wait_send()


def local(ny, nz, tokens, expert_ids, chosen_probs, gate_weight, up_weight, down_weight):
    n = 2 * ny * nz
    per = 2 * nz
    count, ff, width = tokens.shape[0], gate_weight.shape[1], gate_weight.shape[2]
    dma = pltpu.SemaphoreType.DMA
    vmem = pl.BlockSpec(memory_space=pltpu.VMEM)
    anywhere = pl.BlockSpec(memory_space=pl.ANY)
    messages = (ROWS, LANES)
    return pl.pallas_call(
        functools.partial(moe_kernel, ny, nz),
        out_shape=jax.ShapeDtypeStruct(tokens.shape, BF16),
        in_specs=[vmem] * 3 + [anywhere] * 3,
        out_specs=vmem,
        scratch_shapes=[
            pltpu.VMEM((2 * ff, width), BF16),
            pltpu.VMEM((ff, width), BF16),
            pltpu.VMEM((n, count), jnp.int32),
            pltpu.VMEM((n,) + messages, BF16),
            pltpu.VMEM((4, n) + messages, BF16),
            pltpu.VMEM((per * TILE, width), BF16),
            pltpu.VMEM((4, n) + messages, BF16),
            pltpu.VMEM((ny, per) + messages, BF16),
            pltpu.VMEM((2, ny, per) + messages, BF16),
            pltpu.VMEM((ny, per) + messages, BF16),
            pltpu.VMEM((ny, per) + messages, BF16),
            pltpu.VMEM((n,) + messages, BF16),
            pltpu.VMEM((TILES, 4 * count, n * TILE), BF16),
            dma((3,)), dma(()), dma((ny,)), dma(()), dma((2, ny)), dma((ny,)),
            dma(()), dma((ny,)), dma((2, ny)), dma(()), dma(()), dma((2,)),
        ],
        compiler_params=pltpu.CompilerParams(
            collective_id=0, has_side_effects=True, vmem_limit_bytes=60 << 20
        ),
        name="moe",
    )(expert_ids.T, chosen_probs.T, tokens, gate_weight, up_weight, down_weight)


def build(mesh, ny, nz):
    in_specs = (
        P("expert", "dp"),
        P("expert", None),
        P("expert", None),
        P("expert", "dp", None),
        P("expert", "dp", None),
        P("expert", "dp", None),
    )
    return jax.shard_map(
        functools.partial(local, ny, nz),
        mesh=mesh,
        in_specs=in_specs,
        out_specs=P("expert", "dp"),
        check_vma=False,
    )


def solution(mesh):
    return build(mesh, 8, 8)
```

```python
import functools

import jax
import jax.numpy as jnp
from jax import lax
from jax.experimental import pallas as pl
from jax.experimental.pallas import tpu as pltpu
from jax.sharding import PartitionSpec as P

LANES = 128
CAP = 12
TILE = 16
TILES = 3
ROWS = TILE * TILES
F32 = jnp.float32
BF16 = jnp.bfloat16


def wanted_slot(tile, row):
    return jnp.where(row < CAP, row, row - CAP + 4 * tile)


def grid_place(nz):
    e = lax.axis_index("expert")
    core = lax.rem(e, 2)
    z = lax.rem(lax.div(e, 2), nz)
    y = lax.div(e, 2 * nz)
    return e, y, z, core


def peer_at(ring, half, j, dc, sign, place, ny, nz):
    _, y, z, core = place
    dz = j + half * (nz // 2)
    if sign > 0:
        y2, z2 = lax.rem(y + dz + ring, ny), lax.rem(z + dz, nz)
    else:
        y2, z2 = lax.rem(y + 2 * ny - lax.rem(dz + ring, ny), ny), lax.rem(z + nz - dz, nz)
    return (y2 * nz + z2) * 2 + lax.rem(core + dc, 2)


def for_peers(ring, half, place, ny, nz, sign, act):
    for j in range(nz // 2):
        for dc in range(2):
            act(2 * j + dc, peer_at(ring, half, j, dc, sign, place, ny, nz))


def group_of(g):
    ring = lax.div(g, 2)
    return ring, lax.rem(g + ring, 2)


def column_experts(place, ny, nz, wide):
    _, y, z, core = place
    k = lax.broadcasted_iota(jnp.int32, (1, wide), 1) >> 4
    g = k >> (nz.bit_length() - 1)
    ring = g >> 1
    dz = ((k & (nz - 1)) >> 1) + (((g + ring) & 1) << (nz.bit_length() - 2))
    y2, z2 = (y + dz + ring) & (ny - 1), (z + dz) & (nz - 1)
    return (y2 * nz + z2) * 2 + ((core + k) & 1)


def remote(src, dst, send, recv, device):
    return pltpu.make_async_remote_copy(
        src_ref=src,
        dst_ref=dst,
        send_sem=send,
        recv_sem=recv,
        device_id=device,
        device_id_type=pl.DeviceIdType.MESH,
    )


def side_of(x, way):
    return lax.rem(x + 1 + 2 * way, 4)


def route_tables(ids_ref, probs_ref, experts):
    top, tokens = ids_ref.shape
    probs = probs_ref[...]
    route = probs / jnp.sum(probs, axis=0, keepdims=True)
    which = lax.broadcasted_iota(jnp.int32, (experts, tokens), 0)
    chosen = jnp.zeros((experts, tokens), F32)
    weight = jnp.zeros((experts, tokens), F32)
    for k in range(top):
        hit = which == ids_ref[k : k + 1, :]
        chosen = chosen + hit.astype(F32)
        weight = weight + jnp.where(hit, route[k : k + 1, :], 0.0)
    before = lax.broadcasted_iota(jnp.int32, (tokens, tokens), 0)
    after = lax.broadcasted_iota(jnp.int32, (tokens, tokens), 1)
    upper = (before < after).astype(F32).astype(BF16)
    rank = jnp.dot(chosen.astype(BF16), upper, preferred_element_type=F32)
    return jnp.where(chosen > 0.0, rank, -1.0), weight


def pack(slot_ref, tok_ref, packed):
    experts, tokens = slot_ref.shape
    block = min(16, experts)
    row = lax.broadcasted_iota(jnp.int32, (block, TILE, tokens), 1)
    rows2 = lax.broadcasted_iota(jnp.int32, (block, TILE, LANES), 1)

    def step(i, carry):
        start = pl.multiple_of(i * block, block)
        mine = jnp.broadcast_to(slot_ref[pl.ds(start, block), :][:, None, :], (block, TILE, tokens))
        for tile in range(TILES):
            pick = (mine == wanted_slot(tile, row)).astype(F32).astype(BF16)
            pick = pick.reshape(block * TILE, tokens)
            source = jnp.concatenate(
                [tok_ref[:, tile * LANES : (tile + 1) * LANES], tok_ref[:, TILES * LANES :]], axis=1
            )
            got = jnp.dot(pick, source, preferred_element_type=F32)
            main = got[:, :LANES].reshape(block, TILE, LANES)
            rest = got[:, LANES:].reshape(block, TILE, LANES)
            packed[pl.ds(start, block), tile * TILE : (tile + 1) * TILE, :] = jnp.where(
                rows2 < CAP, main, rest
            ).astype(BF16)
        return carry

    lax.fori_loop(0, experts // block, step, 0)


def mixing(slot, weight, columns, mix):
    tokens, experts = slot.shape
    high = weight.astype(BF16)
    rest = (weight - high.astype(F32)).astype(BF16)
    wide = experts * TILE
    line = lax.broadcasted_iota(jnp.int32, (experts, wide), 0)
    spread = (line == columns).astype(F32).astype(BF16)
    slots = jnp.dot(slot.astype(BF16), spread, preferred_element_type=F32).astype(jnp.int32)
    highs = jnp.dot(high, spread, preferred_element_type=F32)
    rests = jnp.dot(rest, spread, preferred_element_type=F32)
    row = lax.broadcasted_iota(jnp.int32, (tokens, wide), 1) & (TILE - 1)
    for tile in range(TILES):
        hit = slots == wanted_slot(tile, row)
        masks = (hit & (row < CAP), hit & (row >= CAP))
        for i, (m, w) in enumerate((m, w) for m in masks for w in (highs, rests)):
            mix[tile, i * tokens : (i + 1) * tokens, :] = jnp.where(m, w, 0.0).astype(BF16)


def combine(mix, ret, start, stop, before):
    tokens = mix.shape[1] // 4
    sums = []
    last = None
    for tile in range(TILES):
        right = ret[start:stop, tile * TILE : (tile + 1) * TILE, :]
        right = right.reshape((stop - start) * TILE, LANES)
        got = jnp.dot(
            mix[tile, :, start * TILE : stop * TILE], right, preferred_element_type=F32
        )
        sums.append(got[:tokens] + got[tokens : 2 * tokens])
        more = got[2 * tokens : 3 * tokens] + got[3 * tokens :]
        last = more if last is None else last + more
    sums.append(last)
    return [a + b for a, b in zip(before, sums)] if before else sums


def apply_expert(arrived, made, start, batch, rows_ref, gate_up, down):
    parts = arrived.shape[0]
    ff = down.shape[0]
    rows = batch * TILE
    half = TILE // 2
    low = lax.broadcasted_iota(jnp.int32, (batch, half, LANES), 1) < half // 2
    for q in range(parts):
        uppers = []
        base = q * (TILES + 1) * LANES
        for tile in range(TILES):
            value = arrived[q, pl.ds(start, batch), tile * TILE : (tile + 1) * TILE, :]
            rows_ref[:, base + tile * LANES : base + (tile + 1) * LANES] = value.reshape(rows, LANES)
            uppers.append(value.astype(F32)[:, half:, :])
        first = jnp.where(low, pltpu.roll(uppers[0], half // 2, 1), uppers[1])
        second = pltpu.roll(uppers[2], half // 2, 1)
        last = jnp.concatenate([first, second], axis=1).reshape(rows, LANES).astype(BF16)
        rows_ref[:, base + TILES * LANES : base + (TILES + 1) * LANES] = last
    dims = (((1,), (1,)), ((), ()))
    both = lax.dot_general(rows_ref[...], gate_up[...], dims, preferred_element_type=F32)
    gate, up = both[:, :ff], both[:, ff:]
    hidden = (gate / (1.0 + jnp.exp(-gate)) * up).astype(BF16)
    for q in range(parts):
        base = q * (TILES + 1) * LANES
        result = jnp.dot(
            hidden, down[:, base : base + (TILES + 1) * LANES], preferred_element_type=F32
        )
        last = result[:, TILES * LANES :].reshape(batch, TILE, LANES)
        fill = (
            pltpu.roll(last[:, :half], half // 2, 1),
            last[:, :half],
            pltpu.roll(last[:, half:], half // 2, 1),
        )
        for tile in range(TILES):
            main = result[:, tile * LANES : (tile + 1) * LANES].reshape(batch, TILE, LANES)
            upper = jnp.where(low, main[:, half:], fill[tile])
            made[q, pl.ds(start, batch), tile * TILE : (tile + 1) * TILE, :] = jnp.concatenate(
                [main[:, :half], upper], axis=1
            ).astype(BF16)


def moe_kernel(
    ny, nz, ids_ref, probs_ref, tok_ref, gate_hbm, up_hbm, down_hbm, out_ref,
    gate_up, down, slot_ref, packed, arrived, rows_ref, made, diag, near, passed, total, ret, mix,
    weight_sem, go_send, go_recv, gather_send, side_recv, far_recv,
    sum_send, diag_recv, near_recv, back_send, back_recv, self_sem,
):
    n = 2 * ny * nz
    per = nz
    groups = n // per
    ff = down.shape[0]
    x = lax.axis_index("dp")
    place = grid_place(nz)
    e = place[0]
    right, left, far = side_of(x, 0), side_of(x, 1), lax.rem(x + 2, 4)

    weights = (
        pltpu.make_async_copy(gate_hbm.at[0], gate_up.at[pl.ds(0, ff)], weight_sem.at[0]),
        pltpu.make_async_copy(up_hbm.at[0], gate_up.at[pl.ds(ff, ff)], weight_sem.at[1]),
        pltpu.make_async_copy(down_hbm.at[0], down, weight_sem.at[2]),
    )
    for copy in weights:
        copy.start()

    barrier = pltpu.get_barrier_semaphore()

    def greet(g, carry):
        def act(i, dest):
            def signal():
                pl.semaphore_signal(
                    barrier,
                    inc=1,
                    device_id={"expert": dest},
                    device_id_type=pl.DeviceIdType.MESH,
                )

            if i == 0:
                pl.when(g > 0)(signal)
            else:
                signal()

        for_peers(*group_of(g), place, ny, nz, 1, act)
        return carry

    for side in (right, left):
        pl.semaphore_signal(
            barrier, inc=1, device_id={"dp": side}, device_id_type=pl.DeviceIdType.MESH
        )
    lax.fori_loop(0, groups, greet, 0)

    slot, weight = route_tables(ids_ref, probs_ref, n)
    slot_ref[...] = slot.astype(jnp.int32)
    pack(slot_ref, tok_ref, packed)
    pl.semaphore_wait(barrier, n + 1)

    def send_out(g, carry):
        def act(i, dest):
            def start():
                remote(
                    packed.at[dest],
                    arrived.at[x, g * per + i],
                    go_send,
                    go_recv.at[g],
                    {"expert": dest},
                ).start()

            if i == 0:
                pl.when(g > 0)(start)
            else:
                start()

        for_peers(*group_of(g), place, ny, nz, 1, act)
        return carry

    own = pltpu.make_async_copy(packed.at[e], arrived.at[x, 0], self_sem.at[0])
    own.start()
    lax.fori_loop(0, groups, send_out, 0)
    mixing(slot.T, weight.T, column_experts(place, ny, nz, n * TILE), mix)
    for copy in weights:
        copy.wait()
    own.wait()

    def got(q, g):
        return arrived.at[q, pl.ds(g * per, per)]

    def part(q, g):
        return made.at[q, pl.ds(g * per, per)]

    def share(g):
        @pl.when(g == 0)
        def _():
            some = arrived.at[x, pl.ds(1, per - 1)]
            remote(some, some, go_send, go_recv.at[0], {"dp": right}).wait_recv()

        @pl.when(g > 0)
        def _():
            remote(got(x, g), got(x, g), go_send, go_recv.at[g], {"dp": right}).wait_recv()

        for way in (0, 1):
            remote(
                got(x, g), got(x, g), gather_send, side_recv.at[way, g], {"dp": side_of(x, way)}
            ).start()

    def share_on(g):
        way = lax.rem(g, 2)
        block = got(side_of(x, 1 - way), g)
        remote(block, block, gather_send, side_recv.at[way, g], {"dp": right}).wait_recv()
        remote(block, block, gather_send, far_recv.at[g], {"dp": side_of(x, way)}).start()

    def work(g):
        way = lax.rem(g, 2)
        block = got(side_of(x, way), g)
        remote(block, block, gather_send, side_recv.at[1 - way, g], {"dp": right}).wait_recv()
        remote(got(far, g), got(far, g), gather_send, far_recv.at[g], {"dp": right}).wait_recv()
        apply_expert(arrived, made, g * per, per, rows_ref, gate_up, down)
        remote(
            part(far, g), diag.at[g], sum_send, diag_recv.at[g], {"dp": side_of(x, way)}
        ).start()
        other = side_of(x, 1 - way)
        remote(
            part(other, g), near.at[1 - way, g], sum_send, near_recv.at[1 - way, g], {"dp": other}
        ).start()

    def sum_on(g):
        way = lax.rem(g, 2)
        dest = side_of(x, way)
        remote(diag.at[g], diag.at[g], sum_send, diag_recv.at[g], {"dp": right}).wait_recv()
        passed[g] = (
            diag[g].astype(F32) + made[dest, pl.ds(g * per, per)].astype(F32)
        ).astype(BF16)
        remote(
            passed.at[g], near.at[way, g], sum_send, near_recv.at[way, g], {"dp": dest}
        ).start()

    def give_back(g):
        for way in (0, 1):
            block = near.at[way, g]
            remote(block, block, sum_send, near_recv.at[way, g], {"dp": right}).wait_recv()
        total[g] = (
            made[x, pl.ds(g * per, per)].astype(F32)
            + near[0, g].astype(F32)
            + near[1, g].astype(F32)
        ).astype(BF16)

        def act(i, dest):
            def start():
                remote(
                    total.at[g, i], ret.at[g * per + i], back_send, back_recv.at[g], {"expert": dest}
                ).start()

            if i == 0:
                pl.when(g > 0)(start)
            else:
                start()

        for_peers(*group_of(g), place, ny, nz, -1, act)

        @pl.when(g == 0)
        def _():
            pltpu.make_async_copy(total.at[0, 0], ret.at[0], self_sem.at[1]).start()

    def step(i, carry):
        for stage, late in ((share, 0), (share_on, 1), (sum_on, 3), (work, 2), (give_back, 4)):

            @pl.when((i >= late) & (i < groups + late))
            def _(stage=stage, late=late):
                stage(i - late)

        return carry

    lax.fori_loop(0, groups + 4, step, 0)
    pltpu.make_async_copy(total.at[0, 0], ret.at[0], self_sem.at[1]).wait()
    early = groups - max(1, groups // 4)
    sums = None
    for start, stop in ((0, early), (early, groups)):
        for g in range(start, stop):
            first = 1 if g == 0 else 0
            block = ret.at[pl.ds(g * per + first, per - first)]
            remote(block, block, back_send, back_recv.at[g], {"dp": right}).wait_recv()
        sums = combine(mix, ret, start * per, stop * per, sums)
    for chunk, value in enumerate(sums):
        out_ref[:, chunk * LANES : (chunk + 1) * LANES] = value.astype(BF16)
    most = ret.at[pl.ds(0, n - 1)]
    remote(most, most, back_send, go_recv.at[0], {"dp": right}).wait_send()
    remote(most, most, go_send, go_recv.at[0], {"dp": right}).wait_send()
    three = made.at[pl.ds(0, 3)]
    remote(three, three, gather_send, go_recv.at[0], {"dp": right}).wait_send()
    remote(three, three, sum_send, go_recv.at[0], {"dp": right}).wait_send()


def local(ny, nz, tokens, expert_ids, chosen_probs, gate_weight, up_weight, down_weight):
    n = 2 * ny * nz
    per = nz
    groups = n // per
    count, ff, width = tokens.shape[0], gate_weight.shape[1], gate_weight.shape[2]
    dma = pltpu.SemaphoreType.DMA
    vmem = pl.BlockSpec(memory_space=pltpu.VMEM)
    anywhere = pl.BlockSpec(memory_space=pl.ANY)
    messages = (ROWS, LANES)
    return pl.pallas_call(
        functools.partial(moe_kernel, ny, nz),
        out_shape=jax.ShapeDtypeStruct(tokens.shape, BF16),
        in_specs=[vmem] * 3 + [anywhere] * 3,
        out_specs=vmem,
        scratch_shapes=[
            pltpu.VMEM((2 * ff, width), BF16),
            pltpu.VMEM((ff, width), BF16),
            pltpu.VMEM((n, count), jnp.int32),
            pltpu.VMEM((n,) + messages, BF16),
            pltpu.VMEM((4, n) + messages, BF16),
            pltpu.VMEM((per * TILE, width), BF16),
            pltpu.VMEM((4, n) + messages, BF16),
            pltpu.VMEM((groups, per) + messages, BF16),
            pltpu.VMEM((2, groups, per) + messages, BF16),
            pltpu.VMEM((groups, per) + messages, BF16),
            pltpu.VMEM((groups, per) + messages, BF16),
            pltpu.VMEM((n,) + messages, BF16),
            pltpu.VMEM((TILES, 4 * count, n * TILE), BF16),
            dma((3,)), dma(()), dma((groups,)), dma(()), dma((2, groups)), dma((groups,)),
            dma(()), dma((groups,)), dma((2, groups)), dma(()), dma((groups,)), dma((2,)),
        ],
        compiler_params=pltpu.CompilerParams(
            collective_id=0, has_side_effects=True, vmem_limit_bytes=60 << 20
        ),
        name="moe",
    )(expert_ids.T, chosen_probs.T, tokens, gate_weight, up_weight, down_weight)


def build(mesh, ny, nz):
    in_specs = (
        P("expert", "dp"),
        P("expert", None),
        P("expert", None),
        P("expert", "dp", None),
        P("expert", "dp", None),
        P("expert", "dp", None),
    )
    return jax.shard_map(
        functools.partial(local, ny, nz),
        mesh=mesh,
        in_specs=in_specs,
        out_specs=P("expert", "dp"),
        check_vma=False,
    )


def solution(mesh):
    return build(mesh, 8, 8)
```

```python
import functools

import jax
import jax.numpy as jnp
from jax import lax
from jax.experimental import pallas as pl
from jax.experimental.pallas import tpu as pltpu
from jax.sharding import PartitionSpec as P

LANES = 128
CAP = 12
TILE = 16
TILES = 3
ROWS = TILE * TILES
F32 = jnp.float32
BF16 = jnp.bfloat16


def wanted_slot(tile, row):
    return jnp.where(row < CAP, row, row - CAP + 4 * tile)


def grid_place(nz):
    e = lax.axis_index("expert")
    core = lax.rem(e, 2)
    z = lax.rem(lax.div(e, 2), nz)
    y = lax.div(e, 2 * nz)
    return e, y, z, core


def peer_at(ring, half, j, dc, sign, place, ny, nz):
    _, y, z, core = place
    dz = 2 * j + half
    if sign > 0:
        y2, z2 = lax.rem(y + dz + ring, ny), lax.rem(z + dz, nz)
    else:
        y2, z2 = lax.rem(y + 2 * ny - lax.rem(dz + ring, ny), ny), lax.rem(z + nz - dz, nz)
    return (y2 * nz + z2) * 2 + lax.rem(core + dc, 2)


def for_peers(ring, half, place, ny, nz, sign, act):
    for j in range(nz // 2):
        for dc in range(2):
            act(2 * j + dc, peer_at(ring, half, j, dc, sign, place, ny, nz))


def straight(g):
    return lax.rem(lax.div(g, 2), 2) == 1


def straight_index(g):
    return 2 * lax.div(g, 4) + lax.rem(g, 2)


def group_of(g):
    ring = lax.div(g, 2)
    return ring, lax.rem(g + ring, 2)


def column_experts(place, ny, nz, wide):
    _, y, z, core = place
    k = lax.broadcasted_iota(jnp.int32, (1, wide), 1) >> 4
    g = k >> (nz.bit_length() - 1)
    ring = g >> 1
    dz = (k & (nz - 2)) + ((g + ring) & 1)
    y2, z2 = (y + dz + ring) & (ny - 1), (z + dz) & (nz - 1)
    return (y2 * nz + z2) * 2 + ((core + k) & 1)


def remote(src, dst, send, recv, device):
    return pltpu.make_async_remote_copy(
        src_ref=src,
        dst_ref=dst,
        send_sem=send,
        recv_sem=recv,
        device_id=device,
        device_id_type=pl.DeviceIdType.MESH,
    )


def side_of(x, way):
    return lax.rem(x + 1 + 2 * way, 4)


def route_tables(ids_ref, probs_ref, experts):
    top, tokens = ids_ref.shape
    probs = probs_ref[...]
    route = probs / jnp.sum(probs, axis=0, keepdims=True)
    which = lax.broadcasted_iota(jnp.int32, (experts, tokens), 0)
    chosen = jnp.zeros((experts, tokens), F32)
    weight = jnp.zeros((experts, tokens), F32)
    for k in range(top):
        hit = which == ids_ref[k : k + 1, :]
        chosen = chosen + hit.astype(F32)
        weight = weight + jnp.where(hit, route[k : k + 1, :], 0.0)
    before = lax.broadcasted_iota(jnp.int32, (tokens, tokens), 0)
    after = lax.broadcasted_iota(jnp.int32, (tokens, tokens), 1)
    upper = (before < after).astype(F32).astype(BF16)
    rank = jnp.dot(chosen.astype(BF16), upper, preferred_element_type=F32)
    return jnp.where(chosen > 0.0, rank, -1.0), weight


def pack(slot_ref, tok_ref, packed):
    experts, tokens = slot_ref.shape
    block = min(16, experts)
    row = lax.broadcasted_iota(jnp.int32, (block, TILE, tokens), 1)
    rows2 = lax.broadcasted_iota(jnp.int32, (block, TILE, LANES), 1)

    def step(i, carry):
        start = pl.multiple_of(i * block, block)
        mine = jnp.broadcast_to(slot_ref[pl.ds(start, block), :][:, None, :], (block, TILE, tokens))
        for tile in range(TILES):
            pick = (mine == wanted_slot(tile, row)).astype(F32).astype(BF16)
            pick = pick.reshape(block * TILE, tokens)
            source = jnp.concatenate(
                [tok_ref[:, tile * LANES : (tile + 1) * LANES], tok_ref[:, TILES * LANES :]], axis=1
            )
            got = jnp.dot(pick, source, preferred_element_type=F32)
            main = got[:, :LANES].reshape(block, TILE, LANES)
            rest = got[:, LANES:].reshape(block, TILE, LANES)
            packed[pl.ds(start, block), tile * TILE : (tile + 1) * TILE, :] = jnp.where(
                rows2 < CAP, main, rest
            ).astype(BF16)
        return carry

    lax.fori_loop(0, experts // block, step, 0)


def mixing(slot, weight, columns, mix):
    tokens, experts = slot.shape
    high = weight.astype(BF16)
    rest = (weight - high.astype(F32)).astype(BF16)
    wide = experts * TILE
    line = lax.broadcasted_iota(jnp.int32, (experts, wide), 0)
    spread = (line == columns).astype(F32).astype(BF16)
    slots = jnp.dot(slot.astype(BF16), spread, preferred_element_type=F32).astype(jnp.int32)
    highs = jnp.dot(high, spread, preferred_element_type=F32)
    rests = jnp.dot(rest, spread, preferred_element_type=F32)
    row = lax.broadcasted_iota(jnp.int32, (tokens, wide), 1) & (TILE - 1)
    for tile in range(TILES):
        hit = slots == wanted_slot(tile, row)
        masks = (hit & (row < CAP), hit & (row >= CAP))
        for i, (m, w) in enumerate((m, w) for m in masks for w in (highs, rests)):
            mix[tile, i * tokens : (i + 1) * tokens, :] = jnp.where(m, w, 0.0).astype(BF16)


def combine(mix, ret, start, stop, before):
    tokens = mix.shape[1] // 4
    sums = []
    last = None
    for tile in range(TILES):
        right = ret[start:stop, tile * TILE : (tile + 1) * TILE, :]
        right = right.reshape((stop - start) * TILE, LANES)
        got = jnp.dot(
            mix[tile, :, start * TILE : stop * TILE], right, preferred_element_type=F32
        )
        sums.append(got[:tokens] + got[tokens : 2 * tokens])
        more = got[2 * tokens : 3 * tokens] + got[3 * tokens :]
        last = more if last is None else last + more
    sums.append(last)
    return [a + b for a, b in zip(before, sums)] if before else sums


def apply_expert(arrived, made, start, batch, rows_ref, gate_up, down):
    parts = arrived.shape[0]
    ff = down.shape[0]
    rows = batch * TILE
    half = TILE // 2
    low = lax.broadcasted_iota(jnp.int32, (batch, half, LANES), 1) < half // 2
    for q in range(parts):
        uppers = []
        base = q * (TILES + 1) * LANES
        for tile in range(TILES):
            value = arrived[q, pl.ds(start, batch), tile * TILE : (tile + 1) * TILE, :]
            rows_ref[:, base + tile * LANES : base + (tile + 1) * LANES] = value.reshape(rows, LANES)
            uppers.append(value.astype(F32)[:, half:, :])
        first = jnp.where(low, pltpu.roll(uppers[0], half // 2, 1), uppers[1])
        second = pltpu.roll(uppers[2], half // 2, 1)
        last = jnp.concatenate([first, second], axis=1).reshape(rows, LANES).astype(BF16)
        rows_ref[:, base + TILES * LANES : base + (TILES + 1) * LANES] = last
    dims = (((1,), (1,)), ((), ()))
    both = lax.dot_general(rows_ref[...], gate_up[...], dims, preferred_element_type=F32)
    gate, up = both[:, :ff], both[:, ff:]
    hidden = (gate / (1.0 + jnp.exp(-gate)) * up).astype(BF16)
    for q in range(parts):
        base = q * (TILES + 1) * LANES
        result = jnp.dot(
            hidden, down[:, base : base + (TILES + 1) * LANES], preferred_element_type=F32
        )
        last = result[:, TILES * LANES :].reshape(batch, TILE, LANES)
        fill = (
            pltpu.roll(last[:, :half], half // 2, 1),
            last[:, :half],
            pltpu.roll(last[:, half:], half // 2, 1),
        )
        for tile in range(TILES):
            main = result[:, tile * LANES : (tile + 1) * LANES].reshape(batch, TILE, LANES)
            upper = jnp.where(low, main[:, half:], fill[tile])
            made[q, pl.ds(start, batch), tile * TILE : (tile + 1) * TILE, :] = jnp.concatenate(
                [main[:, :half], upper], axis=1
            ).astype(BF16)


def moe_kernel(
    ny, nz, ids_ref, probs_ref, tok_ref, gate_hbm, up_hbm, down_hbm, out_ref,
    gate_up, down, slot_ref, packed, arrived, rows_ref, made, diag, near, passed, total, ret, mix,
    far_tok, far_slot, far_packed, route_ref,
    weight_sem, go_send, go_recv, gather_send, side_recv, far_recv,
    sum_send, diag_recv, near_recv, back_send, back_recv, self_sem,
    tok_send, tok_recv, straight_send, relay, relay_recv,
):
    n = 2 * ny * nz
    per = nz
    groups = n // per
    direct = sum(g // 2 % 2 for g in range(groups))
    ff = down.shape[0]
    x = lax.axis_index("dp")
    place = grid_place(nz)
    e = place[0]
    right, left, far = side_of(x, 0), side_of(x, 1), lax.rem(x + 2, 4)

    weights = (
        pltpu.make_async_copy(gate_hbm.at[0], gate_up.at[pl.ds(0, ff)], weight_sem.at[0]),
        pltpu.make_async_copy(up_hbm.at[0], gate_up.at[pl.ds(ff, ff)], weight_sem.at[1]),
        pltpu.make_async_copy(down_hbm.at[0], down, weight_sem.at[2]),
    )
    for copy in weights:
        copy.start()

    barrier = pltpu.get_barrier_semaphore()

    def greet(g, carry):
        def act(i, dest):
            def signal():
                pl.semaphore_signal(
                    barrier,
                    inc=1,
                    device_id={"expert": dest},
                    device_id_type=pl.DeviceIdType.MESH,
                )

            if i == 0:
                pl.when(g > 0)(signal)
            else:
                signal()

        for_peers(*group_of(g), place, ny, nz, 1, act)
        return carry

    for side in (right, left, far):
        pl.semaphore_signal(
            barrier, inc=1, device_id={"dp": side}, device_id_type=pl.DeviceIdType.MESH
        )
    lax.fori_loop(0, groups, greet, 0)

    slot, weight = route_tables(ids_ref, probs_ref, n)
    slot_ref[...] = slot.astype(jnp.int32)
    pack(slot_ref, tok_ref, packed)
    pl.semaphore_wait(barrier, n + 2)
    half = tok_ref.shape[0] // 2
    for way in (0, 1):
        remote(
            tok_ref.at[pl.ds(way * half, half)],
            relay.at[way],
            tok_send,
            relay_recv.at[way],
            {"dp": side_of(x, way)},
        ).start()
    ahead = min(6, groups)

    def send_out(g):
        def act(i, dest):
            def start():
                remote(
                    packed.at[dest],
                    arrived.at[x, g * per + i],
                    go_send,
                    go_recv.at[g],
                    {"expert": dest},
                ).start()

            if i == 0:
                pl.when(g > 0)(start)
            else:
                start()

        for_peers(*group_of(g), place, ny, nz, 1, act)

    def send_straight(g):
        first = straight_index(g) * per

        def act(i, dest):
            remote(
                far_packed.at[first + i],
                arrived.at[far, g * per + i],
                straight_send,
                far_recv.at[g],
                {"expert": dest},
            ).start()

        for_peers(*group_of(g), place, ny, nz, 1, act)

    def pack_far():
        def take(h, carry):
            g = 4 * lax.div(h, 2) + 2 + lax.rem(h, 2)

            def act(i, dest):
                far_slot[pl.ds(h * per + i, 1), :] = slot_ref[pl.ds(dest, 1), :]

            for_peers(*group_of(g), place, ny, nz, 1, act)
            return carry

        lax.fori_loop(0, direct, take, 0)
        remote(far_tok, far_tok, tok_send, tok_recv, {"dp": right}).wait_recv()
        pack(far_slot, far_tok, far_packed)

    own = pltpu.make_async_copy(packed.at[e], arrived.at[x, 0], self_sem.at[0])
    own.start()

    def first_out(g, carry):
        send_out(g)
        return carry

    lax.fori_loop(0, ahead, first_out, 0)
    for way in (0, 1):
        passing = remote(
            relay.at[way],
            far_tok.at[pl.ds(way * half, half)],
            tok_send,
            tok_recv,
            {"dp": side_of(x, way)},
        )
        remote(relay.at[way], relay.at[way], tok_send, relay_recv.at[way], {"dp": right}).wait_recv()
        passing.start()
    route_ref[0] = slot.T
    route_ref[1] = weight.T
    own.wait()
    pack_far()

    def got(q, g):
        return arrived.at[q, pl.ds(g * per, per)]

    def part(q, g):
        return made.at[q, pl.ds(g * per, per)]

    def share(g):
        @pl.when(g == 0)
        def _():
            some = arrived.at[x, pl.ds(1, per - 1)]
            remote(some, some, go_send, go_recv.at[0], {"dp": right}).wait_recv()

        @pl.when(g > 0)
        def _():
            remote(got(x, g), got(x, g), go_send, go_recv.at[g], {"dp": right}).wait_recv()

        for way in (0, 1):
            remote(
                got(x, g), got(x, g), gather_send, side_recv.at[way, g], {"dp": side_of(x, way)}
            ).start()

    def share_on(g):
        way = lax.rem(g, 2)
        block = got(side_of(x, 1 - way), g)
        remote(block, block, gather_send, side_recv.at[way, g], {"dp": right}).wait_recv()

        @pl.when(jnp.logical_not(straight(g)))
        def _():
            remote(block, block, gather_send, far_recv.at[g], {"dp": side_of(x, way)}).start()

    def work(g):
        way = lax.rem(g, 2)
        block = got(side_of(x, way), g)
        remote(block, block, gather_send, side_recv.at[1 - way, g], {"dp": right}).wait_recv()
        remote(got(far, g), got(far, g), gather_send, far_recv.at[g], {"dp": right}).wait_recv()
        apply_expert(arrived, made, g * per, per, rows_ref, gate_up, down)
        remote(
            part(far, g), diag.at[g], sum_send, diag_recv.at[g], {"dp": side_of(x, way)}
        ).start()
        other = side_of(x, 1 - way)
        remote(
            part(other, g), near.at[1 - way, g], sum_send, near_recv.at[1 - way, g], {"dp": other}
        ).start()

    def sum_on(g):
        way = lax.rem(g, 2)
        dest = side_of(x, way)
        remote(diag.at[g], diag.at[g], sum_send, diag_recv.at[g], {"dp": right}).wait_recv()
        passed[g] = (
            diag[g].astype(F32) + made[dest, pl.ds(g * per, per)].astype(F32)
        ).astype(BF16)
        remote(
            passed.at[g], near.at[way, g], sum_send, near_recv.at[way, g], {"dp": dest}
        ).start()

    def give_back(g):
        for way in (0, 1):
            block = near.at[way, g]
            remote(block, block, sum_send, near_recv.at[way, g], {"dp": right}).wait_recv()
        total[g] = (
            made[x, pl.ds(g * per, per)].astype(F32)
            + near[0, g].astype(F32)
            + near[1, g].astype(F32)
        ).astype(BF16)

        def act(i, dest):
            def start():
                remote(
                    total.at[g, i], ret.at[g * per + i], back_send, back_recv.at[g], {"expert": dest}
                ).start()

            if i == 0:
                pl.when(g > 0)(start)
            else:
                start()

        for_peers(*group_of(g), place, ny, nz, -1, act)

        @pl.when(g == 0)
        def _():
            pltpu.make_async_copy(total.at[0, 0], ret.at[0], self_sem.at[1]).start()

    def step(stages, i, carry):
        @pl.when(i < groups)
        def _():
            share(i)

        @pl.when(i < groups - ahead)
        def _():
            send_out(i + ahead)

        @pl.when((i < groups - 2) & straight(i + 2))
        def _():
            send_straight(i + 2)

        for stage, late in stages:

            @pl.when((i >= late) & (i < groups + late))
            def _(stage=stage, late=late):
                stage(i - late)

        return carry

    first = ((share_on, 1),)
    every = ((share_on, 1), (sum_on, 6), (work, 4), (give_back, 8))
    lax.fori_loop(0, 4, functools.partial(step, first), 0)
    mixing(route_ref[0], route_ref[1], column_experts(place, ny, nz, n * TILE), mix)
    for copy in weights:
        copy.wait()
    lax.fori_loop(4, groups + 8, functools.partial(step, every), 0)
    pltpu.make_async_copy(total.at[0, 0], ret.at[0], self_sem.at[1]).wait()
    early = groups - max(1, groups // 4)
    sums = None
    for start, stop in ((0, early), (early, groups)):
        for g in range(start, stop):
            first = 1 if g == 0 else 0
            block = ret.at[pl.ds(g * per + first, per - first)]
            remote(block, block, back_send, back_recv.at[g], {"dp": right}).wait_recv()
        sums = combine(mix, ret, start * per, stop * per, sums)
    for chunk, value in enumerate(sums):
        out_ref[:, chunk * LANES : (chunk + 1) * LANES] = value.astype(BF16)
    most = ret.at[pl.ds(0, n - 1)]
    remote(most, most, back_send, go_recv.at[0], {"dp": right}).wait_send()
    remote(most, most, go_send, go_recv.at[0], {"dp": right}).wait_send()
    for _ in (0, 1):
        remote(far_tok, far_tok, tok_send, tok_recv, {"dp": right}).wait_send()
    some = packed.at[pl.ds(0, direct * per)]
    remote(some, some, straight_send, go_recv.at[0], {"dp": right}).wait_send()
    some = packed.at[pl.ds(0, n - direct * per)]
    remote(some, some, gather_send, go_recv.at[0], {"dp": right}).wait_send()
    two = made.at[pl.ds(0, 2)]
    remote(two, two, gather_send, go_recv.at[0], {"dp": right}).wait_send()
    three = made.at[pl.ds(0, 3)]
    remote(three, three, sum_send, go_recv.at[0], {"dp": right}).wait_send()


def local(ny, nz, tokens, expert_ids, chosen_probs, gate_weight, up_weight, down_weight):
    n = 2 * ny * nz
    per = nz
    groups = n // per
    direct = sum(g // 2 % 2 for g in range(groups))
    count, ff, width = tokens.shape[0], gate_weight.shape[1], gate_weight.shape[2]
    dma = pltpu.SemaphoreType.DMA
    vmem = pl.BlockSpec(memory_space=pltpu.VMEM)
    anywhere = pl.BlockSpec(memory_space=pl.ANY)
    messages = (ROWS, LANES)
    return pl.pallas_call(
        functools.partial(moe_kernel, ny, nz),
        out_shape=jax.ShapeDtypeStruct(tokens.shape, BF16),
        in_specs=[vmem] * 3 + [anywhere] * 3,
        out_specs=vmem,
        scratch_shapes=[
            pltpu.VMEM((2 * ff, width), BF16),
            pltpu.VMEM((ff, width), BF16),
            pltpu.VMEM((n, count), jnp.int32),
            pltpu.VMEM((n,) + messages, BF16),
            pltpu.VMEM((4, n) + messages, BF16),
            pltpu.VMEM((per * TILE, width), BF16),
            pltpu.VMEM((4, n) + messages, BF16),
            pltpu.VMEM((groups, per) + messages, BF16),
            pltpu.VMEM((2, groups, per) + messages, BF16),
            pltpu.VMEM((groups, per) + messages, BF16),
            pltpu.VMEM((groups, per) + messages, BF16),
            pltpu.VMEM((n,) + messages, BF16),
            pltpu.VMEM((TILES, 4 * count, n * TILE), BF16),
            pltpu.VMEM(tokens.shape, BF16),
            pltpu.VMEM((direct * per, count), jnp.int32),
            pltpu.VMEM((direct * per,) + messages, BF16),
            pltpu.VMEM((2, count, n), F32),
            dma((3,)), dma(()), dma((groups,)), dma(()), dma((2, groups)), dma((groups,)),
            dma(()), dma((groups,)), dma((2, groups)), dma(()), dma((groups,)), dma((2,)),
            dma(()), dma(()), dma(()),
            pltpu.VMEM((2, count // 2, tokens.shape[1]), BF16), dma((2,)),
        ],
        compiler_params=pltpu.CompilerParams(
            collective_id=0, has_side_effects=True, vmem_limit_bytes=60 << 20
        ),
        name="moe",
    )(expert_ids.T, chosen_probs.T, tokens, gate_weight, up_weight, down_weight)


def build(mesh, ny, nz):
    in_specs = (
        P("expert", "dp"),
        P("expert", None),
        P("expert", None),
        P("expert", "dp", None),
        P("expert", "dp", None),
        P("expert", "dp", None),
    )
    return jax.shard_map(
        functools.partial(local, ny, nz),
        mesh=mesh,
        in_specs=in_specs,
        out_specs=P("expert", "dp"),
        check_vma=False,
    )


def solution(mesh):
    return build(mesh, 8, 8)
```

```python
import functools

import jax
import jax.numpy as jnp
from jax import lax
from jax.experimental import pallas as pl
from jax.experimental.pallas import tpu as pltpu
from jax.sharding import PartitionSpec as P

LANES = 128
CAP = 12
TILE = 16
TILES = 3
ROWS = TILE * TILES
F32 = jnp.float32
BF16 = jnp.bfloat16


def wanted_slot(tile, row):
    return jnp.where(row < CAP, row, row - CAP + 4 * tile)


def grid_place(nz):
    e = lax.axis_index("expert")
    core = lax.rem(e, 2)
    z = lax.rem(lax.div(e, 2), nz)
    y = lax.div(e, 2 * nz)
    return e, y, z, core


def peer_at(ring, half, j, dc, sign, place, ny, nz):
    _, y, z, core = place
    dz = 2 * j + half
    if sign > 0:
        y2, z2 = lax.rem(y + dz + ring, ny), lax.rem(z + dz, nz)
    else:
        y2, z2 = lax.rem(y + 2 * ny - lax.rem(dz + ring, ny), ny), lax.rem(z + nz - dz, nz)
    return (y2 * nz + z2) * 2 + lax.rem(core + dc, 2)


def for_peers(ring, half, place, ny, nz, sign, act):
    for j in range(nz // 2):
        for dc in range(2):
            act(2 * j + dc, peer_at(ring, half, j, dc, sign, place, ny, nz))


def straight(g):
    return lax.rem(lax.div(g, 2), 2) == 1


def straight_index(g):
    return 2 * lax.div(g, 4) + lax.rem(g, 2)


def group_of(g):
    ring = lax.div(g, 2)
    return ring, lax.rem(g + ring, 2)


def column_experts(place, ny, nz, wide):
    _, y, z, core = place
    k = lax.broadcasted_iota(jnp.int32, (1, wide), 1) >> 4
    g = k >> (nz.bit_length() - 1)
    ring = g >> 1
    dz = (k & (nz - 2)) + ((g + ring) & 1)
    y2, z2 = (y + dz + ring) & (ny - 1), (z + dz) & (nz - 1)
    return (y2 * nz + z2) * 2 + ((core + k) & 1)


def remote(src, dst, send, recv, device):
    return pltpu.make_async_remote_copy(
        src_ref=src,
        dst_ref=dst,
        send_sem=send,
        recv_sem=recv,
        device_id=device,
        device_id_type=pl.DeviceIdType.MESH,
    )


def side_of(x, way):
    return lax.rem(x + 1 + 2 * way, 4)


def route_tables(ids_ref, probs_ref, experts):
    top, tokens = ids_ref.shape
    probs = probs_ref[...]
    route = probs / jnp.sum(probs, axis=0, keepdims=True)
    which = lax.broadcasted_iota(jnp.int32, (experts, tokens), 0)
    chosen = jnp.zeros((experts, tokens), F32)
    weight = jnp.zeros((experts, tokens), F32)
    for k in range(top):
        hit = which == ids_ref[k : k + 1, :]
        chosen = chosen + hit.astype(F32)
        weight = weight + jnp.where(hit, route[k : k + 1, :], 0.0)
    before = lax.broadcasted_iota(jnp.int32, (tokens, tokens), 0)
    after = lax.broadcasted_iota(jnp.int32, (tokens, tokens), 1)
    upper = (before < after).astype(F32).astype(BF16)
    rank = jnp.dot(chosen.astype(BF16), upper, preferred_element_type=F32)
    return jnp.where(chosen > 0.0, rank, -1.0), weight


def pack(slot_ref, tok_ref, packed):
    experts, tokens = slot_ref.shape
    block = min(16, experts)
    row = lax.broadcasted_iota(jnp.int32, (block, TILE, tokens), 1)
    rows2 = lax.broadcasted_iota(jnp.int32, (block, TILE, LANES), 1)

    def step(i, carry):
        start = pl.multiple_of(i * block, block)
        mine = jnp.broadcast_to(slot_ref[pl.ds(start, block), :][:, None, :], (block, TILE, tokens))
        for tile in range(TILES):
            pick = (mine == wanted_slot(tile, row)).astype(F32).astype(BF16)
            pick = pick.reshape(block * TILE, tokens)
            source = jnp.concatenate(
                [tok_ref[:, tile * LANES : (tile + 1) * LANES], tok_ref[:, TILES * LANES :]], axis=1
            )
            got = jnp.dot(pick, source, preferred_element_type=F32)
            main = got[:, :LANES].reshape(block, TILE, LANES)
            rest = got[:, LANES:].reshape(block, TILE, LANES)
            packed[pl.ds(start, block), tile * TILE : (tile + 1) * TILE, :] = jnp.where(
                rows2 < CAP, main, rest
            ).astype(BF16)
        return carry

    lax.fori_loop(0, experts // block, step, 0)


def mixing(slot, weight, columns, mix):
    tokens, experts = slot.shape
    high = weight.astype(BF16)
    rest = (weight - high.astype(F32)).astype(BF16)
    wide = experts * TILE
    line = lax.broadcasted_iota(jnp.int32, (experts, wide), 0)
    spread = (line == columns).astype(F32).astype(BF16)
    slots = jnp.dot(slot.astype(BF16), spread, preferred_element_type=F32).astype(jnp.int32)
    highs = jnp.dot(high, spread, preferred_element_type=F32)
    rests = jnp.dot(rest, spread, preferred_element_type=F32)
    row = lax.broadcasted_iota(jnp.int32, (tokens, wide), 1) & (TILE - 1)
    for tile in range(TILES):
        hit = slots == wanted_slot(tile, row)
        masks = (hit & (row < CAP), hit & (row >= CAP))
        for i, (m, w) in enumerate((m, w) for m in masks for w in (highs, rests)):
            mix[tile, i * tokens : (i + 1) * tokens, :] = jnp.where(m, w, 0.0).astype(BF16)


def combine(mix, ret, start, stop, before):
    tokens = mix.shape[1] // 4
    sums = []
    last = None
    for tile in range(TILES):
        right = ret[start:stop, tile * TILE : (tile + 1) * TILE, :]
        right = right.reshape((stop - start) * TILE, LANES)
        got = jnp.dot(
            mix[tile, :, start * TILE : stop * TILE], right, preferred_element_type=F32
        )
        sums.append(got[:tokens] + got[tokens : 2 * tokens])
        more = got[2 * tokens : 3 * tokens] + got[3 * tokens :]
        last = more if last is None else last + more
    sums.append(last)
    return [a + b for a, b in zip(before, sums)] if before else sums


def apply_expert(arrived, made, start, batch, rows_ref, gate_up, down):
    parts = arrived.shape[0]
    ff = down.shape[0]
    rows = batch * TILE
    half = TILE // 2
    low = lax.broadcasted_iota(jnp.int32, (batch, half, LANES), 1) < half // 2
    for q in range(parts):
        uppers = []
        base = q * (TILES + 1) * LANES
        for tile in range(TILES):
            value = arrived[q, pl.ds(start, batch), tile * TILE : (tile + 1) * TILE, :]
            rows_ref[:, base + tile * LANES : base + (tile + 1) * LANES] = value.reshape(rows, LANES)
            uppers.append(value.astype(F32)[:, half:, :])
        first = jnp.where(low, pltpu.roll(uppers[0], half // 2, 1), uppers[1])
        second = pltpu.roll(uppers[2], half // 2, 1)
        last = jnp.concatenate([first, second], axis=1).reshape(rows, LANES).astype(BF16)
        rows_ref[:, base + TILES * LANES : base + (TILES + 1) * LANES] = last
    dims = (((1,), (1,)), ((), ()))
    both = lax.dot_general(rows_ref[...], gate_up[...], dims, preferred_element_type=F32)
    gate, up = both[:, :ff], both[:, ff:]
    hidden = (gate / (1.0 + jnp.exp(-gate)) * up).astype(BF16)
    for q in range(parts):
        base = q * (TILES + 1) * LANES
        result = jnp.dot(
            hidden, down[:, base : base + (TILES + 1) * LANES], preferred_element_type=F32
        )
        last = result[:, TILES * LANES :].reshape(batch, TILE, LANES)
        fill = (
            pltpu.roll(last[:, :half], half // 2, 1),
            last[:, :half],
            pltpu.roll(last[:, half:], half // 2, 1),
        )
        for tile in range(TILES):
            main = result[:, tile * LANES : (tile + 1) * LANES].reshape(batch, TILE, LANES)
            upper = jnp.where(low, main[:, half:], fill[tile])
            made[q, pl.ds(start, batch), tile * TILE : (tile + 1) * TILE, :] = jnp.concatenate(
                [main[:, :half], upper], axis=1
            ).astype(BF16)


def moe_kernel(
    ny, nz, ids_ref, probs_ref, tok_ref, gate_hbm, up_hbm, down_hbm, out_ref,
    gate_up, down, slot_ref, packed, arrived, rows_ref, made, diag, near, passed, total, ret, mix,
    far_tok, far_slot, far_packed, route_ref,
    weight_sem, go_send, go_recv, gather_send, side_recv, far_recv,
    sum_send, diag_recv, near_recv, back_send, back_recv, self_sem,
    tok_send, tok_recv, straight_send, relay, relay_recv,
):
    n = 2 * ny * nz
    per = nz
    groups = n // per
    direct = sum(g // 2 % 2 for g in range(groups))
    ff = down.shape[0]
    x = lax.axis_index("dp")
    place = grid_place(nz)
    e = place[0]
    right, left, far = side_of(x, 0), side_of(x, 1), lax.rem(x + 2, 4)

    weights = (
        pltpu.make_async_copy(gate_hbm.at[0], gate_up.at[pl.ds(0, ff)], weight_sem.at[0]),
        pltpu.make_async_copy(up_hbm.at[0], gate_up.at[pl.ds(ff, ff)], weight_sem.at[1]),
        pltpu.make_async_copy(down_hbm.at[0], down, weight_sem.at[2]),
    )
    for copy in weights:
        copy.start()

    barrier = pltpu.get_barrier_semaphore()

    def greet(g, carry):
        def act(i, dest):
            def signal():
                pl.semaphore_signal(
                    barrier,
                    inc=1,
                    device_id={"expert": dest},
                    device_id_type=pl.DeviceIdType.MESH,
                )

            if i == 0:
                pl.when(g > 0)(signal)
            else:
                signal()

        for_peers(*group_of(g), place, ny, nz, 1, act)
        return carry

    for side in (right, left, far):
        pl.semaphore_signal(
            barrier, inc=1, device_id={"dp": side}, device_id_type=pl.DeviceIdType.MESH
        )
    lax.fori_loop(0, groups, greet, 0)

    slot, weight = route_tables(ids_ref, probs_ref, n)
    slot_ref[...] = slot.astype(jnp.int32)
    pack(slot_ref, tok_ref, packed)
    pl.semaphore_wait(barrier, n + 2)
    half = tok_ref.shape[0] // 2
    for way in (0, 1):
        remote(
            tok_ref.at[pl.ds(way * half, half)],
            relay.at[way],
            tok_send,
            relay_recv.at[way],
            {"dp": side_of(x, way)},
        ).start()
    ahead = min(4, groups)

    def send_out(g):
        def act(i, dest):
            def start():
                remote(
                    packed.at[dest],
                    arrived.at[x, g * per + i],
                    go_send,
                    go_recv.at[g],
                    {"expert": dest},
                ).start()

            if i == 0:
                pl.when(g > 0)(start)
            else:
                start()

        for_peers(*group_of(g), place, ny, nz, 1, act)

    def send_straight(g):
        first = straight_index(g) * per

        def act(i, dest):
            remote(
                far_packed.at[first + i],
                arrived.at[far, g * per + i],
                straight_send,
                far_recv.at[g],
                {"expert": dest},
            ).start()

        for_peers(*group_of(g), place, ny, nz, 1, act)

    def pack_far():
        def take(h, carry):
            g = 4 * lax.div(h, 2) + 2 + lax.rem(h, 2)

            def act(i, dest):
                far_slot[pl.ds(h * per + i, 1), :] = slot_ref[pl.ds(dest, 1), :]

            for_peers(*group_of(g), place, ny, nz, 1, act)
            return carry

        lax.fori_loop(0, direct, take, 0)
        remote(far_tok, far_tok, tok_send, tok_recv, {"dp": right}).wait_recv()
        pack(far_slot, far_tok, far_packed)

    own = pltpu.make_async_copy(packed.at[e], arrived.at[x, 0], self_sem.at[0])
    own.start()

    def first_out(g, carry):
        send_out(g)
        return carry

    lax.fori_loop(0, ahead, first_out, 0)
    for way in (0, 1):
        passing = remote(
            relay.at[way],
            far_tok.at[pl.ds(way * half, half)],
            tok_send,
            tok_recv,
            {"dp": side_of(x, way)},
        )
        remote(relay.at[way], relay.at[way], tok_send, relay_recv.at[way], {"dp": right}).wait_recv()
        passing.start()
    route_ref[0] = slot.T
    route_ref[1] = weight.T
    own.wait()
    pack_far()

    def got(q, g):
        return arrived.at[q, pl.ds(g * per, per)]

    def part(q, g):
        return made.at[q, pl.ds(g * per, per)]

    def share(g):
        @pl.when(g == 0)
        def _():
            some = arrived.at[x, pl.ds(1, per - 1)]
            remote(some, some, go_send, go_recv.at[0], {"dp": right}).wait_recv()

        @pl.when(g > 0)
        def _():
            remote(got(x, g), got(x, g), go_send, go_recv.at[g], {"dp": right}).wait_recv()

        for way in (0, 1):
            remote(
                got(x, g), got(x, g), gather_send, side_recv.at[way, g], {"dp": side_of(x, way)}
            ).start()

    def share_on(g):
        way = lax.rem(g, 2)
        block = got(side_of(x, 1 - way), g)
        remote(block, block, gather_send, side_recv.at[way, g], {"dp": right}).wait_recv()

        @pl.when(jnp.logical_not(straight(g)))
        def _():
            remote(block, block, gather_send, far_recv.at[g], {"dp": side_of(x, way)}).start()

    def work(g):
        way = lax.rem(g, 2)
        block = got(side_of(x, way), g)
        remote(block, block, gather_send, side_recv.at[1 - way, g], {"dp": right}).wait_recv()
        remote(got(far, g), got(far, g), gather_send, far_recv.at[g], {"dp": right}).wait_recv()
        apply_expert(arrived, made, g * per, per, rows_ref, gate_up, down)
        remote(
            part(far, g), diag.at[g], sum_send, diag_recv.at[g], {"dp": side_of(x, way)}
        ).start()
        other = side_of(x, 1 - way)
        remote(
            part(other, g), near.at[1 - way, g], sum_send, near_recv.at[1 - way, g], {"dp": other}
        ).start()

    def sum_on(g):
        way = lax.rem(g, 2)
        dest = side_of(x, way)
        remote(diag.at[g], diag.at[g], sum_send, diag_recv.at[g], {"dp": right}).wait_recv()
        passed[g] = (
            diag[g].astype(F32) + made[dest, pl.ds(g * per, per)].astype(F32)
        ).astype(BF16)
        remote(
            passed.at[g], near.at[way, g], sum_send, near_recv.at[way, g], {"dp": dest}
        ).start()

    def give_back(g):
        for way in (0, 1):
            block = near.at[way, g]
            remote(block, block, sum_send, near_recv.at[way, g], {"dp": right}).wait_recv()
        total[g] = (
            made[x, pl.ds(g * per, per)].astype(F32)
            + near[0, g].astype(F32)
            + near[1, g].astype(F32)
        ).astype(BF16)

        def act(i, dest):
            def start():
                remote(
                    total.at[g, i], ret.at[g * per + i], back_send, back_recv.at[g], {"expert": dest}
                ).start()

            if i == 0:
                pl.when(g > 0)(start)
            else:
                start()

        for_peers(*group_of(g), place, ny, nz, -1, act)

        @pl.when(g == 0)
        def _():
            pltpu.make_async_copy(total.at[0, 0], ret.at[0], self_sem.at[1]).start()

    def step(stages, i, carry):
        @pl.when(i < groups)
        def _():
            share(i)

        @pl.when(i < groups - ahead)
        def _():
            send_out(i + ahead)

        @pl.when((i < groups - 2) & straight(i + 2))
        def _():
            send_straight(i + 2)

        for stage, late in stages:

            @pl.when((i >= late) & (i < groups + late))
            def _(stage=stage, late=late):
                stage(i - late)

        return carry

    first = ((share_on, 1),)
    every = ((share_on, 1), (sum_on, 6), (work, 4), (give_back, 8))
    lax.fori_loop(0, 4, functools.partial(step, first), 0)
    mixing(route_ref[0], route_ref[1], column_experts(place, ny, nz, n * TILE), mix)
    for copy in weights:
        copy.wait()
    lax.fori_loop(4, groups + 8, functools.partial(step, every), 0)
    pltpu.make_async_copy(total.at[0, 0], ret.at[0], self_sem.at[1]).wait()
    early = groups - max(1, groups // 4)
    sums = None
    for start, stop in ((0, early), (early, groups)):
        for g in range(start, stop):
            first = 1 if g == 0 else 0
            block = ret.at[pl.ds(g * per + first, per - first)]
            remote(block, block, back_send, back_recv.at[g], {"dp": right}).wait_recv()
        sums = combine(mix, ret, start * per, stop * per, sums)
    for chunk, value in enumerate(sums):
        out_ref[:, chunk * LANES : (chunk + 1) * LANES] = value.astype(BF16)
    most = ret.at[pl.ds(0, n - 1)]
    remote(most, most, back_send, go_recv.at[0], {"dp": right}).wait_send()
    remote(most, most, go_send, go_recv.at[0], {"dp": right}).wait_send()
    for _ in (0, 1):
        remote(far_tok, far_tok, tok_send, tok_recv, {"dp": right}).wait_send()
    some = packed.at[pl.ds(0, direct * per)]
    remote(some, some, straight_send, go_recv.at[0], {"dp": right}).wait_send()
    some = packed.at[pl.ds(0, n - direct * per)]
    remote(some, some, gather_send, go_recv.at[0], {"dp": right}).wait_send()
    two = made.at[pl.ds(0, 2)]
    remote(two, two, gather_send, go_recv.at[0], {"dp": right}).wait_send()
    three = made.at[pl.ds(0, 3)]
    remote(three, three, sum_send, go_recv.at[0], {"dp": right}).wait_send()


def local(ny, nz, tokens, expert_ids, chosen_probs, gate_weight, up_weight, down_weight):
    n = 2 * ny * nz
    per = nz
    groups = n // per
    direct = sum(g // 2 % 2 for g in range(groups))
    count, ff, width = tokens.shape[0], gate_weight.shape[1], gate_weight.shape[2]
    dma = pltpu.SemaphoreType.DMA
    vmem = pl.BlockSpec(memory_space=pltpu.VMEM)
    anywhere = pl.BlockSpec(memory_space=pl.ANY)
    messages = (ROWS, LANES)
    return pl.pallas_call(
        functools.partial(moe_kernel, ny, nz),
        out_shape=jax.ShapeDtypeStruct(tokens.shape, BF16),
        in_specs=[vmem] * 3 + [anywhere] * 3,
        out_specs=vmem,
        scratch_shapes=[
            pltpu.VMEM((2 * ff, width), BF16),
            pltpu.VMEM((ff, width), BF16),
            pltpu.VMEM((n, count), jnp.int32),
            pltpu.VMEM((n,) + messages, BF16),
            pltpu.VMEM((4, n) + messages, BF16),
            pltpu.VMEM((per * TILE, width), BF16),
            pltpu.VMEM((4, n) + messages, BF16),
            pltpu.VMEM((groups, per) + messages, BF16),
            pltpu.VMEM((2, groups, per) + messages, BF16),
            pltpu.VMEM((groups, per) + messages, BF16),
            pltpu.VMEM((groups, per) + messages, BF16),
            pltpu.VMEM((n,) + messages, BF16),
            pltpu.VMEM((TILES, 4 * count, n * TILE), BF16),
            pltpu.VMEM(tokens.shape, BF16),
            pltpu.VMEM((direct * per, count), jnp.int32),
            pltpu.VMEM((direct * per,) + messages, BF16),
            pltpu.VMEM((2, count, n), F32),
            dma((3,)), dma(()), dma((groups,)), dma(()), dma((2, groups)), dma((groups,)),
            dma(()), dma((groups,)), dma((2, groups)), dma(()), dma((groups,)), dma((2,)),
            dma(()), dma(()), dma(()),
            pltpu.VMEM((2, count // 2, tokens.shape[1]), BF16), dma((2,)),
        ],
        compiler_params=pltpu.CompilerParams(
            collective_id=0, has_side_effects=True, vmem_limit_bytes=60 << 20
        ),
        name="moe",
    )(expert_ids.T, chosen_probs.T, tokens, gate_weight, up_weight, down_weight)


def build(mesh, ny, nz):
    in_specs = (
        P("expert", "dp"),
        P("expert", None),
        P("expert", None),
        P("expert", "dp", None),
        P("expert", "dp", None),
        P("expert", "dp", None),
    )
    return jax.shard_map(
        functools.partial(local, ny, nz),
        mesh=mesh,
        in_specs=in_specs,
        out_specs=P("expert", "dp"),
        check_vma=False,
    )


def solution(mesh):
    return build(mesh, 8, 8)
```
